32 devices in a mesh: section: 2 (over x), seq: 16 (over z, y, core).
Axes of the slice: x: 2, y: 2, z: 4, core: 2. Of those that a mesh axis runs over, the one named last changes fastest.
Arguments:
- queries: bfloat16 [2, 2048, 3072], P('section', 'seq'), may hold values from -60 to 60
- packed_key_value: bfloat16 [2, 2048, 1024], P('section', 'seq'), may hold values from -6 to 6
- incoming: bfloat16 [2, 2048, 3072], P('section', 'seq'), may hold values from -6 to 6
- loss_grad: bfloat16 [2048, 3072], P('seq'), may hold values from -6 to 6
- global_blocks: int32 [2, 2], P('section'), may hold values from 0 to 31
- random_blocks: int32 [2, 32, 4, 3], P('section'), may hold values from 0 to 31, as said below
Outputs:
- d_queries: bfloat16 [2, 2048, 3072], P('section', 'seq')
- d_key_value: bfloat16 [2, 2048, 1024], P('section', 'seq')
The draws below stay inside these ranges and needn't reach their ends.
Inputs may be any that keep to these rules, and one draw needn't show every extreme that they name: `random_blocks`: the random blocks of a query block lie among the blocks held by the seq index that holds the query block and the indices just before and after it.
All inputs are finite; a program needn't handle non-finite values.
Results may differ from the reference program's by a relative error of at most 0.006.
Values may be sent and summed in bfloat16 or wider, within the bound.
No kernel may reach another device: no remote copies, remote signals or barrier semaphores. Data moves between devices by JAX's collectives and lax.ppermute only.
A program may use at most 64 MiB of HBM per device.

```python
import math
import jax
import jax.numpy as jnp
from jax import lax

HQ = 24
KEY_HEADS = 4
HEAD_SIZE = 128
BLOCK_TOKENS = 64
GLOBAL_BLOCKS = 2
RANDOM_BLOCKS = 3
TOK_DEV = 128
GROUP_HEADS = 6
SEQUENCE_TOKENS = 2048
N_SECTION = 2


def base_pairs(key):
    sub_key = jax.random.fold_in(key, 101)
    complete_shape = (N_SECTION, SEQUENCE_TOKENS, 2 * KEY_HEADS * HEAD_SIZE)
    block_pairs = jnp.clip(jax.random.normal(sub_key, complete_shape, jnp.float32), -6.0, 6.0)
    return block_pairs


def draw_packed_key_value(key, part):
    return base_pairs(key).astype(jnp.bfloat16)


def draw_queries(key, part):
    complete_shape = (N_SECTION, SEQUENCE_TOKENS, HQ * HEAD_SIZE)
    sub_key = jax.random.fold_in(key, 202)
    values_out = jnp.clip(jax.random.normal(sub_key, complete_shape, jnp.float32), -6.0, 6.0)
    return values_out.astype(jnp.bfloat16)


def draw_random_blocks(key, part):
    local_block_count = TOK_DEV // BLOCK_TOKENS
    every_block = SEQUENCE_TOKENS // BLOCK_TOKENS
    seq_count = SEQUENCE_TOKENS // TOK_DEV
    device_ids = jnp.arange(every_block, dtype=jnp.int32) // local_block_count
    lower = jnp.maximum(device_ids - 1, 0) * local_block_count
    upper = jnp.minimum(device_ids + 2, seq_count) * local_block_count
    random_integers = jax.random.randint(jax.random.fold_in(key, 404), (N_SECTION, every_block, KEY_HEADS, RANDOM_BLOCKS), 0, 1 << 20)
    spans = (upper - lower)[None, :, None, None]
    return (lower[None, :, None, None] + random_integers % spans).astype(jnp.int32)


def plant(result, key, low, top_value):
    longest = result.shape.index(max(result.shape))
    spots = []
    for shift in (0, 1):
        where = [jax.random.randint(jax.random.fold_in(key, axis), (), 0, length) for axis, length in enumerate(result.shape)]
        where[longest] = (where[longest] + shift) % result.shape[longest]
        spots.append(tuple(where))
    return result.at[spots[0]].set(low).at[spots[1]].set(top_value)


def level_of(stream_key, extent, shards, least, largest):
    factor_of = 1.0
    for axis_at, blocks in shards:
        steps = jax.random.uniform(jax.random.fold_in(jax.random.fold_in(stream_key, 6), axis_at), (blocks,), jnp.float32, least / len(shards), largest / len(shards))
        factor_of = factor_of * jnp.repeat(jnp.exp(steps), extent[axis_at] // blocks).reshape((-1,) + (1,) * (len(extent) - 1 - axis_at))
    return factor_of


def gaussian(stream_key, shape, deviation, limit, shards=(), kind=jnp.bfloat16):
    gain = level_of(stream_key, shape, shards, -0.22, 0.18) if shards else 1.0
    array = jax.random.normal(stream_key, shape, jnp.float32) * deviation * gain
    return jnp.minimum(jnp.maximum(array, -limit), limit).astype(kind)


def setup_inputs(seed: int = 0) -> dict:
    key_list = jax.random.split(jax.random.key(seed), 7)
    queries = draw_queries(jax.random.fold_in(key_list[6], 71), 0)
    packed_key_value = draw_packed_key_value(jax.random.fold_in(key_list[6], 71), 0)
    incoming = gaussian(key_list[2], (N_SECTION, SEQUENCE_TOKENS, HQ * HEAD_SIZE), 1.0, 6.0, ((0, 2), (1, 16)))
    loss_grad = gaussian(key_list[3], (SEQUENCE_TOKENS, HQ * HEAD_SIZE), 1.0, 6.0, ((0, 16),))
    global_blocks = plant(jax.random.randint(key_list[4], (N_SECTION, GLOBAL_BLOCKS), 0, SEQUENCE_TOKENS // BLOCK_TOKENS), jax.random.fold_in(key_list[4], 1), 0, (SEQUENCE_TOKENS // BLOCK_TOKENS) - 1).astype(jnp.int32)
    random_blocks = draw_random_blocks(jax.random.fold_in(key_list[6], 71), 0)
    return {"queries": queries, "packed_key_value": packed_key_value, "incoming": incoming, "loss_grad": loss_grad, "global_blocks": global_blocks, "random_blocks": random_blocks}


def section_grads(section_args):
    queries, packed_key_value, output_gradient, global_block_index, random_block_index = section_args
    score_scale = 1.0 / math.sqrt(HEAD_SIZE)
    every_block = SEQUENCE_TOKENS // BLOCK_TOKENS
    block_ids = jnp.arange(every_block, dtype=jnp.int32)
    window_blocks = block_ids[:, None] + jnp.arange(-1, 2, dtype=jnp.int32)[None, :]
    usable = jnp.concatenate([(window_blocks >= 0) & (window_blocks < every_block), jnp.ones((every_block, GLOBAL_BLOCKS + RANDOM_BLOCKS), dtype=bool)], 1)
    window_blocks = jnp.clip(window_blocks, 0, every_block - 1).astype(jnp.int32)
    global_key_tile = jnp.broadcast_to(global_block_index.astype(jnp.int32)[None, None, :], (KEY_HEADS, every_block, GLOBAL_BLOCKS))
    key_block_index = jnp.concatenate([jnp.broadcast_to(window_blocks[None], (KEY_HEADS, every_block, 3)), global_key_tile, jnp.transpose(random_block_index, (1, 0, 2)).astype(jnp.int32)], 2)
    key_mask = jnp.repeat(usable, BLOCK_TOKENS, axis=1)
    query_group_rows = queries.reshape(every_block, BLOCK_TOKENS, KEY_HEADS, GROUP_HEADS, HEAD_SIZE).transpose(2, 0, 1, 3, 4)
    gradient_group_rows = output_gradient.reshape(every_block, BLOCK_TOKENS, KEY_HEADS, GROUP_HEADS, HEAD_SIZE).transpose(2, 0, 1, 3, 4)
    paired_groups = packed_key_value.reshape(every_block, BLOCK_TOKENS, 2, KEY_HEADS, HEAD_SIZE).transpose(3, 0, 1, 2, 4)

    def one_group(group_args):
        index_g, query_grouped, gradient_grouped, pairs_g = group_args
        selected = pairs_g[index_g]
        key_row_block = selected[:, :, :, 0].reshape(every_block, -1, HEAD_SIZE).astype(jnp.float32)
        value_row_block = selected[:, :, :, 1].reshape(every_block, -1, HEAD_SIZE).astype(jnp.float32)
        query_wide = query_grouped.astype(jnp.float32)
        gradient_wide = gradient_grouped.astype(jnp.float32)
        logit_scores = jnp.einsum('elmi,eti->emlt', query_wide, key_row_block) * score_scale
        logit_scores = jnp.where(key_mask[:, None, None, :], logit_scores, -1e+30)
        row_max = lax.optimization_barrier(jnp.max(logit_scores, axis=-1, keepdims=True))
        weights_raw = jnp.exp(logit_scores - row_max)
        probs = weights_raw / lax.optimization_barrier(jnp.sum(weights_raw, axis=-1, keepdims=True))
        probability_lowbits = probs.astype(jnp.bfloat16)
        probability_gradient = jnp.einsum('elmi,eti->emlt', gradient_wide, value_row_block)
        row_delta = lax.optimization_barrier(jnp.sum(probs * probability_gradient, axis=-1, keepdims=True))
        score_gradient = (probs * (probability_gradient - row_delta) * score_scale).astype(jnp.bfloat16)
        scores_wide = score_gradient.astype(jnp.float32)
        query_gradient = jnp.einsum('yzmu,yup->ymzp', scores_wide, key_row_block)
        key_gradient = jnp.einsum('xapt,xpag->xtg', scores_wide, query_wide)
        value_gradient = jnp.einsum('xapt,xpag->xtg', probability_lowbits.astype(jnp.float32), gradient_wide)
        paired = jnp.stack([key_gradient, value_gradient], 2).reshape(-1, BLOCK_TOKENS, 2, HEAD_SIZE)
        summed = jnp.zeros((every_block, BLOCK_TOKENS, 2, HEAD_SIZE), jnp.float32).at[index_g.reshape(-1)].add(paired)
        return (query_gradient, summed)
    grad_query_all, reduced_total = lax.map(one_group, (key_block_index, query_group_rows, gradient_group_rows, paired_groups))
    d_q = grad_query_all.transpose(1, 2, 0, 3, 4).reshape(SEQUENCE_TOKENS, HQ * HEAD_SIZE).astype(jnp.bfloat16)
    key_value_gradient = reduced_total.transpose(1, 2, 3, 0, 4).reshape(SEQUENCE_TOKENS, 2 * KEY_HEADS * HEAD_SIZE).astype(jnp.bfloat16)
    return (d_q, key_value_gradient)

def reference(queries, packed_key_value, incoming, loss_grad, global_blocks, random_blocks):
    d_out_all = jnp.concatenate([incoming[1:], loss_grad[None]], 0)
    d_queries, d_key_value = lax.map(section_grads, (queries, packed_key_value, d_out_all, global_blocks, random_blocks))
    return (d_queries, d_key_value)
```

```python
import functools
import math

import jax
import jax.numpy as jnp
from jax import lax
from jax.experimental import pallas as pl
from jax.experimental.pallas import tpu as pltpu
from jax.sharding import PartitionSpec as P

HQ = 24
KEY_HEADS = 4
HEAD_SIZE = 128
BLOCK_TOKENS = 64
GLOBAL_BLOCKS = 2
GROUP_HEADS = 6
SCALE = 1.0 / math.sqrt(HEAD_SIZE)
LOG2E = math.log2(math.e)
NEG = -1e30
NT = (((1,), (1,)), ((), ()))
NN = (((1,), (0,)), ((), ()))
TN = (((0,), (0,)), ((), ()))


def dot(a, b, dims):
    return lax.dot_general(a, b, dims, preferred_element_type=jnp.float32)


def exchange(x, pairs):
    return lax.ppermute(x, "seq", pairs)


def attention_kernel(
    flag_ref,
    bias_ref,
    q_ref,
    shifted_ref,
    loss_ref,
    own_k, own_v, on_k, on_v, off_k, off_v, glob_k, glob_v,
    dq_ref,
    g_own,
    g_on,
    g_off,
    g_glob,
):
    g = pl.program_id(0)
    toks = q_ref.shape[0]
    nb = toks // BLOCK_TOKENS
    rows_e = GROUP_HEADS * BLOCK_TOKENS
    ncand = bias_ref.shape[1] // KEY_HEADS

    def rows_of(ref):
        parts = [
            ref[e * BLOCK_TOKENS : (e + 1) * BLOCK_TOKENS, h * HEAD_SIZE : (h + 1) * HEAD_SIZE]
            for e in range(nb)
            for h in range(GROUP_HEADS)
        ]
        return jnp.concatenate(parts, 0)

    qg = rows_of(q_ref)
    dog = jnp.where(flag_ref[0] == 1, rows_of(loss_ref), rows_of(shifted_ref))
    keys = jnp.concatenate([own_k[...], on_k[...], off_k[...], glob_k[...]], 0)
    vals = jnp.concatenate([own_v[...], on_v[...], off_v[...], glob_v[...]], 0)
    dq_cols = []
    p_cols = []
    ds_cols = []
    for e in range(nb):
        q_e = qg[e * rows_e : (e + 1) * rows_e]
        do_e = dog[e * rows_e : (e + 1) * rows_e]
        s = dot(keys, q_e, NT)
        dp = dot(vals, do_e, NT)
        t = jnp.concatenate(
            [
                s[j * BLOCK_TOKENS : (j + 1) * BLOCK_TOKENS] * (SCALE * LOG2E)
                + bias_ref[e, g * ncand + j]
                for j in range(ncand)
            ],
            0,
        )
        m = jnp.max(t, axis=0, keepdims=True)
        w = jnp.exp2(t - m)
        inv = 1.0 / jnp.sum(w, axis=0, keepdims=True)
        p = w * inv
        delta = jnp.sum(p * dp, axis=0, keepdims=True)
        p_cols.append(p.astype(jnp.bfloat16))
        ds_cols.append((p * (dp - delta) * SCALE).astype(jnp.bfloat16))
    p_half = jnp.concatenate(p_cols, 1)
    ds_half = jnp.concatenate(ds_cols, 1)
    dq = dot(keys, ds_half, TN).T
    for e in range(nb):
        for h in range(GROUP_HEADS):
            r = e * rows_e + h * BLOCK_TOKENS
            dq_ref[e * BLOCK_TOKENS : (e + 1) * BLOCK_TOKENS, h * HEAD_SIZE : (h + 1) * HEAD_SIZE] = (
                dq[r : r + BLOCK_TOKENS].astype(dq_ref.dtype)
            )
    for i, grad in enumerate((dot(ds_half, qg, NN), dot(p_half, dog, NN))):
        g_own[i] = grad[:toks]
        g_on[i] = grad[toks : 2 * toks].astype(g_on.dtype)
        g_off[i] = grad[2 * toks : 3 * toks].astype(g_off.dtype)
        for b in range(GLOBAL_BLOCKS):
            r = 3 * toks + b * BLOCK_TOKENS
            g_glob[b, i] = grad[r : r + BLOCK_TOKENS].astype(g_glob.dtype)


def attention(flag, bias, queries, shifted, loss, own, on, off, glob):
    toks = queries.shape[0]
    bf = jnp.bfloat16
    wide = pl.BlockSpec((toks, GROUP_HEADS * HEAD_SIZE), lambda g: (0, g))
    k_of = pl.BlockSpec((toks, HEAD_SIZE), lambda g: (0, g))
    v_of = pl.BlockSpec((toks, HEAD_SIZE), lambda g: (0, g + KEY_HEADS))
    glob_rows = GLOBAL_BLOCKS * BLOCK_TOKENS
    gk_of = pl.BlockSpec((glob_rows, HEAD_SIZE), lambda g: (0, g))
    gv_of = pl.BlockSpec((glob_rows, HEAD_SIZE), lambda g: (0, g + KEY_HEADS))
    smem = pl.BlockSpec(memory_space=pltpu.SMEM)
    width = KEY_HEADS * HEAD_SIZE
    pair = pl.BlockSpec((2, toks, HEAD_SIZE), lambda g: (0, 0, g))
    quad = pl.BlockSpec((GLOBAL_BLOCKS, 2, BLOCK_TOKENS, HEAD_SIZE), lambda g: (0, 0, 0, g))
    return pl.pallas_call(
        attention_kernel,
        grid=(KEY_HEADS,),
        in_specs=[smem, smem, wide, wide, wide, k_of, v_of, k_of, v_of, k_of, v_of, gk_of, gv_of],
        out_specs=[wide, pair, pair, pair, quad],
        out_shape=[
            jax.ShapeDtypeStruct((toks, HQ * HEAD_SIZE), bf),
            jax.ShapeDtypeStruct((2, toks, width), jnp.float32),
            jax.ShapeDtypeStruct((2, toks, width), bf),
            jax.ShapeDtypeStruct((2, toks, width), bf),
            jax.ShapeDtypeStruct((GLOBAL_BLOCKS, 2, BLOCK_TOKENS, width), bf),
        ],
        compiler_params=pltpu.CompilerParams(vmem_limit_bytes=40 << 20),
        name="attention",
    )(flag, bias, queries, shifted, loss, own, own, on, on, off, off, glob, glob)


def finish_kernel(where_ref, g_own, r_on, r_off, r_glob, out_ref):
    toks = g_own.shape[1]
    nb = toks // BLOCK_TOKENS
    width = g_own.shape[2]
    for i in range(2):
        for s in range(nb):
            rows = slice(s * BLOCK_TOKENS, (s + 1) * BLOCK_TOKENS)
            total = (
                g_own[i, rows] + r_on[i, rows].astype(jnp.float32) + r_off[i, rows].astype(jnp.float32)
            )
            for b in range(GLOBAL_BLOCKS):
                total = total + jnp.where(
                    where_ref[b] == s, r_glob[b, i].astype(jnp.float32), 0.0
                )
            out_ref[rows, i * width : (i + 1) * width] = total.astype(out_ref.dtype)


def finish(where, g_own, r_on, r_off, r_glob):
    toks, width = g_own.shape[1:]
    vmem = pl.BlockSpec(memory_space=pltpu.VMEM)
    return pl.pallas_call(
        finish_kernel,
        in_specs=[pl.BlockSpec(memory_space=pltpu.SMEM)] + [vmem] * 4,
        out_specs=vmem,
        out_shape=jax.ShapeDtypeStruct((toks, 2 * width), jnp.bfloat16),
        name="finish",
    )(where, g_own, r_on, r_off, r_glob)


def body(queries, packed_key_value, incoming, loss_grad, global_blocks, random_blocks):
    toks = queries.shape[1]
    nb = toks // BLOCK_TOKENS
    sections = lax.axis_size("section")
    peers = lax.axis_size("seq")
    bits = peers.bit_length() - 1
    assert peers == 1 << bits and bits >= 1
    pos = lax.axis_index("seq")
    core = pos % 2
    is_last = lax.axis_index("section") == sections - 1

    twin = [(i, i ^ 1) for i in range(peers)]
    side = [(i, i + 1) for i in range(1, peers - 1, 2)]
    side = side + [(j, i) for i, j in side]
    orders = (list(range(1, bits)), list(range(2, bits)) + [1])
    hops = [
        [(i, i ^ (1 << orders[i % 2][r])) for i in range(peers)] for r in range(bits - 1)
    ]

    shifted = lax.ppermute(incoming[0], "section", [(i, i - 1) for i in range(1, sections)])
    own = packed_key_value[0]
    on = exchange(own, twin)
    off = exchange(own, side)

    glob_ids = global_blocks[0]
    owner = glob_ids // nb
    slot = glob_ids % nb
    mine_owner = jnp.where(core == 0, owner[0], owner[1])
    mine_slot = jnp.where(core == 0, slot[0], slot[1])
    row = mine_slot * BLOCK_TOKENS
    from_own = lax.dynamic_slice_in_dim(own, row, BLOCK_TOKENS, 0)
    from_on = lax.dynamic_slice_in_dim(on, row, BLOCK_TOKENS, 0)
    held = jnp.where(mine_owner == pos, from_own, jnp.where(mine_owner == pos + 1 - 2 * core, from_on, 0))
    for hop in hops:
        held = held + exchange(held, hop)
    other = exchange(held, twin)
    glob = jnp.where(core == 0, jnp.concatenate([held, other], 0), jnp.concatenate([other, held], 0))

    on_pos = pos + 1 - 2 * core
    off_pos = pos - 1 + 2 * core
    step = jnp.arange(nb, dtype=jnp.int32)
    cand_ids = jnp.concatenate([pos * nb + step, on_pos * nb + step, off_pos * nb + step])
    block_ids = pos * nb + step
    own_random = lax.dynamic_slice_in_dim(random_blocks[0], pos * nb, nb, 0)
    listed = jnp.sum(
        (own_random[:, :, None, :] == cand_ids[None, None, :, None]).astype(jnp.float32), -1
    )
    inside = (cand_ids >= 0) & (cand_ids < peers * nb)
    window = (jnp.abs(cand_ids[None, :] - block_ids[:, None]) <= 1) & inside[None, :]
    times = listed + window[:, None, :].astype(jnp.float32)
    bias = jnp.where(times > 0, jnp.log2(jnp.maximum(times, 1.0)), NEG)
    bias = jnp.concatenate([bias, jnp.zeros((nb, KEY_HEADS, GLOBAL_BLOCKS), jnp.float32)], 2)
    bias = bias.reshape(nb, -1)
    flag = is_last.astype(jnp.int32).reshape(1)

    dq, g_own, g_on, g_off, g_glob = attention(
        flag, bias, queries[0], shifted, loss_grad, own, on, off, glob
    )

    keep = jnp.where(core == 0, g_glob[0], g_glob[1])
    give = jnp.where(core == 0, g_glob[1], g_glob[0])
    total = keep.astype(jnp.float32) + exchange(give, twin).astype(jnp.float32)
    for hop in hops:
        total = total + exchange(total.astype(jnp.bfloat16), hop).astype(jnp.float32)
    half = total.astype(jnp.bfloat16)
    half_other = exchange(half, twin)
    r_glob = jnp.where(core == 0, jnp.stack([half, half_other]), jnp.stack([half_other, half]))
    r_on = exchange(g_on, twin)
    r_off = exchange(g_off, side)
    where = jnp.where(owner == pos, slot, -1).astype(jnp.int32)
    out = finish(where, g_own, r_on, r_off, r_glob)
    return (dq[None], out[None])


def solution(mesh):
    in_specs = (
        P("section", "seq", None),
        P("section", "seq", None),
        P("section", "seq", None),
        P("seq", None),
        P("section", None),
        P("section", None, None, None),
    )
    out_specs = (P("section", "seq", None), P("section", "seq", None))
    return jax.shard_map(body, mesh=mesh, in_specs=in_specs, out_specs=out_specs, check_vma=False)
```

```python
import functools
import math

import jax
import jax.numpy as jnp
from jax import lax
from jax.experimental import pallas as pl
from jax.experimental.pallas import tpu as pltpu
from jax.sharding import PartitionSpec as P

HQ = 24
KEY_HEADS = 4
HEAD_SIZE = 128
BLOCK_TOKENS = 64
GLOBAL_BLOCKS = 2
GROUP_HEADS = 6
SCALE = 1.0 / math.sqrt(HEAD_SIZE)
LOG2E = math.log2(math.e)
NEG = -1e30
WIDTH = KEY_HEADS * HEAD_SIZE
ROWS_E = GROUP_HEADS * BLOCK_TOKENS
GLOB_ROWS = GLOBAL_BLOCKS * BLOCK_TOKENS
NT = (((1,), (1,)), ((), ()))
NN = (((1,), (0,)), ((), ()))
TN = (((0,), (0,)), ((), ()))
F32 = jnp.float32
BF = jnp.bfloat16
VMEM = pl.BlockSpec(memory_space=pltpu.VMEM)
SMEM = pl.BlockSpec(memory_space=pltpu.SMEM)


def dot(a, b, dims):
    return lax.dot_general(a, b, dims, preferred_element_type=F32)


def call(kernel, name, ins, outs, args, flops):
    return pl.pallas_call(
        kernel,
        in_specs=ins,
        out_specs=[VMEM] * len(outs),
        out_shape=outs,
        compiler_params=pltpu.CompilerParams(vmem_limit_bytes=24 << 20),
        cost_estimate=pl.CostEstimate(flops=flops, bytes_accessed=flops // 500, transcendentals=0),
        name=name,
    )(*args)


def shape(*dims, dtype=F32):
    return jax.ShapeDtypeStruct(dims, dtype)


def group_rows(ref, g):
    toks = ref.shape[0]
    parts = []
    for e in range(toks // BLOCK_TOKENS):
        for h in range(GROUP_HEADS):
            c = (g * GROUP_HEADS + h) * HEAD_SIZE
            parts.append(ref[e * BLOCK_TOKENS : (e + 1) * BLOCK_TOKENS, c : c + HEAD_SIZE])
    return jnp.concatenate(parts, 0)


def stacked(refs, c):
    return jnp.concatenate([ref[:, c : c + HEAD_SIZE] for ref in refs], 0)


def at_last_section():
    return lax.axis_index("section") == lax.axis_size("section") - 1


def pick_kernel(ids_ref, own_ref, on_ref, out_ref):
    nb = own_ref.shape[0] // BLOCK_TOKENS
    pos = lax.axis_index("seq")
    core = lax.rem(pos, 2)
    block = ids_ref[0, core]
    owner = lax.div(block, nb)
    row = pl.multiple_of(lax.rem(block, nb) * BLOCK_TOKENS, BLOCK_TOKENS)
    twin = pos + 1 - 2 * core
    mine = owner == pos
    theirs = owner == twin

    @pl.when(mine)
    def _():
        out_ref[...] = own_ref[pl.ds(row, BLOCK_TOKENS), :]

    @pl.when(theirs)
    def _():
        out_ref[...] = on_ref[pl.ds(row, BLOCK_TOKENS), :]

    @pl.when(jnp.logical_not(mine | theirs))
    def _():
        out_ref[...] = jnp.zeros_like(out_ref)


def local_kernel(bias_ref, q_ref, own_ref, on_ref, off_ref, w_ref, stat_ref):
    toks = q_ref.shape[0]
    nb = toks // BLOCK_TOKENS
    ncand = 3 * nb
    for g in range(KEY_HEADS):
        keys = stacked((own_ref, on_ref, off_ref), g * HEAD_SIZE)
        s = dot(keys, group_rows(q_ref, g), NT)
        for e in range(nb):
            cols = slice(e * ROWS_E, (e + 1) * ROWS_E)
            t = jnp.concatenate(
                [
                    s[j * BLOCK_TOKENS : (j + 1) * BLOCK_TOKENS, cols] * (SCALE * LOG2E)
                    + bias_ref[e, g * ncand + j]
                    for j in range(ncand)
                ],
                0,
            )
            m = jnp.max(t, axis=0, keepdims=True)
            w = jnp.exp2(t - m)
            w_ref[g, :, cols] = w
            stat_ref[g, 0:1, cols] = m
            stat_ref[g, 1:2, cols] = jnp.sum(w, axis=0, keepdims=True)


def global_kernel(
    q_ref, shifted_ref, loss_ref, own_ref, on_ref, off_ref, held_ref, other_ref, w_ref, stat_ref,
    dp_ref, ds_ref, out_stat_ref, keep_ref, give_ref, do_ref,
):
    last = at_last_section()

    @pl.when(last)
    def _():
        do_ref[...] = loss_ref[...]

    @pl.when(jnp.logical_not(last))
    def _():
        do_ref[...] = shifted_ref[...]

    for g in range(KEY_HEADS):
        kc = g * HEAD_SIZE
        vc = WIDTH + kc
        qg = group_rows(q_ref, g)
        dog = group_rows(do_ref, g)
        t = dot(stacked((held_ref, other_ref), kc), qg, NT) * (SCALE * LOG2E)
        dpg = dot(stacked((held_ref, other_ref), vc), dog, NT)
        dpl = dot(stacked((own_ref, on_ref, off_ref), vc), dog, NT)
        dp_ref[g] = dpl
        partial_delta = jnp.sum(w_ref[g] * dpl, axis=0, keepdims=True)
        m_local = stat_ref[g, 0:1, :]
        m = jnp.maximum(m_local, jnp.max(t, axis=0, keepdims=True))
        shrink = jnp.exp2(m_local - m)
        w = jnp.exp2(t - m)
        total = shrink * stat_ref[g, 1:2, :] + jnp.sum(w, axis=0, keepdims=True)
        inv = 1.0 / total
        p = w * inv
        local_factor = shrink * inv
        delta = local_factor * partial_delta + jnp.sum(p * dpg, axis=0, keepdims=True)
        ds = (p * (dpg - delta) * SCALE).astype(BF)
        ds_ref[g] = ds
        out_stat_ref[g, 0:1, :] = local_factor
        out_stat_ref[g, 1:2, :] = delta
        cols = slice(kc, kc + HEAD_SIZE)
        for i, grad in enumerate((dot(ds, qg, NN), dot(p.astype(BF), dog, NN))):
            keep_ref[i, :, cols] = grad[:BLOCK_TOKENS]
            give_ref[i, :, cols] = grad[BLOCK_TOKENS:].astype(BF)


def rest_kernel(
    q_ref, do_ref, own_ref, on_ref, off_ref, held_ref, other_ref, w_ref, dp_ref, ds_ref, stat_ref,
    dq_ref, g_own, g_on, g_off,
):
    toks = q_ref.shape[0]
    for g in range(KEY_HEADS):
        kc = g * HEAD_SIZE
        keys = stacked((own_ref, on_ref, off_ref, held_ref, other_ref), kc)
        p = w_ref[g] * stat_ref[g, 0:1, :]
        ds = (p * (dp_ref[g] - stat_ref[g, 1:2, :]) * SCALE).astype(BF)
        ds_all = jnp.concatenate([ds, ds_ref[g]], 0)
        dq = dot(keys, ds_all, TN).T
        for e in range(toks // BLOCK_TOKENS):
            for h in range(GROUP_HEADS):
                r = e * ROWS_E + h * BLOCK_TOKENS
                c = (g * GROUP_HEADS + h) * HEAD_SIZE
                dq_ref[e * BLOCK_TOKENS : (e + 1) * BLOCK_TOKENS, c : c + HEAD_SIZE] = (
                    dq[r : r + BLOCK_TOKENS].astype(BF)
                )
        cols = slice(kc, kc + HEAD_SIZE)
        grads = (dot(ds, group_rows(q_ref, g), NN), dot(p.astype(BF), group_rows(do_ref, g), NN))
        for i, grad in enumerate(grads):
            g_own[i, :, cols] = grad[:toks]
            g_on[i, :, cols] = grad[toks : 2 * toks].astype(BF)
            g_off[i, :, cols] = grad[2 * toks :].astype(BF)


def finish_kernel(ids_ref, g_own, r_on, r_off, half_ref, half_other_ref, out_ref):
    toks = g_own.shape[1]
    nb = toks // BLOCK_TOKENS
    pos = lax.axis_index("seq")
    core = lax.rem(pos, 2)
    places = []
    for which in (core, 1 - core):
        block = ids_ref[0, which]
        places.append(jnp.where(lax.div(block, nb) == pos, lax.rem(block, nb), -1))
    for i in range(2):
        for s in range(nb):
            rows = slice(s * BLOCK_TOKENS, (s + 1) * BLOCK_TOKENS)
            total = g_own[i, rows] + r_on[i, rows].astype(F32) + r_off[i, rows].astype(F32)
            for place, ref in zip(places, (half_ref, half_other_ref)):
                total = total + jnp.where(place == s, ref[i].astype(F32), 0.0)
            out_ref[rows, i * WIDTH : (i + 1) * WIDTH] = total.astype(BF)


def list_bias(random_table, pos, peers, nb):
    core = pos % 2
    step = jnp.arange(nb, dtype=jnp.int32)
    holders = (pos, pos + 1 - 2 * core, pos - 1 + 2 * core)
    cand_ids = jnp.concatenate([h * nb + step for h in holders])
    block_ids = pos * nb + step
    own_random = lax.dynamic_slice_in_dim(random_table, pos * nb, nb, 0)
    listed = jnp.sum((own_random[:, :, None, :] == cand_ids[None, None, :, None]).astype(F32), -1)
    inside = (cand_ids >= 0) & (cand_ids < peers * nb)
    window = (jnp.abs(cand_ids[None, :] - block_ids[:, None]) <= 1) & inside[None, :]
    times = listed + window[:, None, :].astype(F32)
    bias = jnp.where(times > 0, jnp.log2(jnp.maximum(times, 1.0)), NEG)
    return bias.reshape(nb, -1)


def body(queries, packed_key_value, incoming, loss_grad, global_blocks, random_blocks):
    toks = queries.shape[1]
    nb = toks // BLOCK_TOKENS
    rows = nb * ROWS_E
    sections = lax.axis_size("section")
    peers = lax.axis_size("seq")
    bits = peers.bit_length() - 1
    assert peers == 1 << bits and bits >= 1
    pos = lax.axis_index("seq")

    twin = [(i, i ^ 1) for i in range(peers)]
    side = [(i, i + 1) for i in range(1, peers - 1, 2)]
    side = side + [(j, i) for i, j in side]
    orders = (list(range(1, bits)), list(range(2, bits)) + [1])
    hops = [
        [(i, i ^ (1 << orders[i % 2][r])) for i in range(peers)] for r in range(bits - 1)
    ]
    exchange = lambda x, pairs: lax.ppermute(x, "seq", pairs)

    q = queries[0]
    own = packed_key_value[0]
    on = exchange(own, twin)
    shifted = lax.ppermute(incoming[0], "section", [(i, i - 1) for i in range(1, sections)])
    (held,) = call(
        pick_kernel, "pick", [SMEM, VMEM, VMEM], [shape(BLOCK_TOKENS, own.shape[1], dtype=BF)],
        (global_blocks, own, on), 10**6,
    )
    off = exchange(own, side)
    for hop in hops:
        held = held + exchange(held, hop)
    other = exchange(held, twin)

    bias = list_bias(random_blocks[0], pos, peers, nb)
    near = (own, on, off)
    w, stats = call(
        local_kernel, "local", [SMEM] + [VMEM] * 4,
        [shape(KEY_HEADS, 3 * toks, rows), shape(KEY_HEADS, 8, rows)],
        (bias, q) + near, 3 * 10**9,
    )
    dp, ds, stats, keep, give, d_out = call(
        global_kernel, "globals", [VMEM] * 10,
        [
            shape(KEY_HEADS, 3 * toks, rows),
            shape(KEY_HEADS, GLOB_ROWS, rows, dtype=BF),
            shape(KEY_HEADS, 8, rows),
            shape(2, BLOCK_TOKENS, WIDTH),
            shape(2, BLOCK_TOKENS, WIDTH, dtype=BF),
            shape(*q.shape, dtype=BF),
        ],
        (q, shifted, loss_grad) + near + (held, other, w, stats), 3 * 10**9,
    )
    total = keep + exchange(give, twin).astype(F32)
    dq, g_own, g_on, g_off = call(
        rest_kernel, "rest", [VMEM] * 11,
        [
            shape(*q.shape, dtype=BF),
            shape(2, toks, WIDTH),
            shape(2, toks, WIDTH, dtype=BF),
            shape(2, toks, WIDTH, dtype=BF),
        ],
        (q, d_out) + near + (held, other, w, dp, ds, stats), 5 * 10**9,
    )
    r_on = exchange(g_on, twin)
    r_off = exchange(g_off, side)
    for hop in hops:
        total = total + exchange(total.astype(BF), hop).astype(F32)
    half = total.astype(BF)
    half_other = exchange(half, twin)
    (out,) = call(
        finish_kernel, "finish", [SMEM] + [VMEM] * 5, [shape(*own.shape, dtype=BF)],
        (global_blocks, g_own, r_on, r_off, half, half_other), 10**6,
    )
    return (dq[None], out[None])


def solution(mesh):
    in_specs = (
        P("section", "seq", None),
        P("section", "seq", None),
        P("section", "seq", None),
        P("seq", None),
        P("section", None),
        P("section", None, None, None),
    )
    out_specs = (P("section", "seq", None), P("section", "seq", None))
    return jax.shard_map(body, mesh=mesh, in_specs=in_specs, out_specs=out_specs, check_vma=False)
```

```python
import math

import jax
import jax.numpy as jnp
from jax import lax
from jax.experimental import pallas as pl
from jax.experimental.pallas import tpu as pltpu
from jax.sharding import PartitionSpec as P


KEY_HEADS = 4
HEAD_SIZE = 128
BLOCK_TOKENS = 64
GLOBAL_BLOCKS = 2
GROUP_HEADS = 6
SCALE = 1.0 / math.sqrt(HEAD_SIZE)
LOG2E = math.log2(math.e)
NEG = -1e30
WIDTH = KEY_HEADS * HEAD_SIZE
ROWS_E = GROUP_HEADS * BLOCK_TOKENS
GLOB_ROWS = GLOBAL_BLOCKS * BLOCK_TOKENS
NT = (((1,), (1,)), ((), ()))
NN = (((1,), (0,)), ((), ()))
TN = (((0,), (0,)), ((), ()))
F32 = jnp.float32
BF = jnp.bfloat16
HBM = pl.BlockSpec(memory_space=pltpu.HBM)
VMEM = pl.BlockSpec(memory_space=pltpu.VMEM)
SMEM = pl.BlockSpec(memory_space=pltpu.SMEM)


def dot(a, b, dims):
    return lax.dot_general(a, b, dims, preferred_element_type=F32)


def call(kernel, ins, outs, args, flops, scratch=()):
    return pl.pallas_call(
        kernel,
        in_specs=ins,
        out_specs=[VMEM] * len(outs),
        out_shape=outs,
        scratch_shapes=scratch,
        compiler_params=pltpu.CompilerParams(vmem_limit_bytes=24 << 20),
        cost_estimate=pl.CostEstimate(flops=flops, bytes_accessed=flops // 500, transcendentals=0),
    )(*args)


def shape(*dims, dtype=F32):
    return jax.ShapeDtypeStruct(dims, dtype)


def group_rows(ref, g):
    toks = ref.shape[0]
    parts = []
    for e in range(toks // BLOCK_TOKENS):
        for h in range(GROUP_HEADS):
            c = (g * GROUP_HEADS + h) * HEAD_SIZE
            parts.append(ref[e * BLOCK_TOKENS : (e + 1) * BLOCK_TOKENS, c : c + HEAD_SIZE])
    return jnp.concatenate(parts, 0)


def stacked(refs, c):
    return jnp.concatenate([ref[:, c : c + HEAD_SIZE] for ref in refs], 0)


def at_last_section():
    return lax.axis_index("section") == lax.axis_size("section") - 1


def load_kernel(a_ref, b_ref, c_ref, a_out, b_out, c_out, sems):
    copies = [
        pltpu.make_async_copy(src, dst, sems.at[i])
        for i, (src, dst) in enumerate(((a_ref, a_out), (b_ref, b_out), (c_ref, c_out)))
    ]
    for copy in copies:
        copy.start()
    for copy in copies:
        copy.wait()


def pick_kernel(table_ref, own_ref, on_ref, out_ref, sem):
    pos = lax.axis_index("seq")
    core = lax.rem(pos, 2)
    owner = table_ref[0, core]
    row = pl.multiple_of(table_ref[1, core] * BLOCK_TOKENS, BLOCK_TOKENS)
    mine = owner == pos
    theirs = owner == pos + 1 - 2 * core

    @pl.when(mine)
    def _():
        copy = pltpu.make_async_copy(own_ref.at[pl.ds(row, BLOCK_TOKENS)], out_ref, sem)
        copy.start()
        copy.wait()

    @pl.when(theirs)
    def _():
        out_ref[...] = on_ref[pl.ds(row, BLOCK_TOKENS), :]

    @pl.when(jnp.logical_not(mine | theirs))
    def _():
        out_ref[...] = jnp.zeros_like(out_ref)


def local_kernel(bias_ref, q_ref, own_ref, on_ref, off_ref, w_ref, stat_ref):
    toks = q_ref.shape[0]
    nb = toks // BLOCK_TOKENS
    ncand = 3 * nb
    for g in range(KEY_HEADS):
        keys = stacked((own_ref, on_ref, off_ref), g * HEAD_SIZE)
        s = dot(keys, group_rows(q_ref, g), NT)
        for e in range(nb):
            cols = slice(e * ROWS_E, (e + 1) * ROWS_E)
            t = jnp.concatenate(
                [
                    s[j * BLOCK_TOKENS : (j + 1) * BLOCK_TOKENS, cols] * (SCALE * LOG2E)
                    + bias_ref[e, g * ncand + j]
                    for j in range(ncand)
                ],
                0,
            )
            m = jnp.max(t, axis=0, keepdims=True)
            w = jnp.exp2(t - m)
            w_ref[g, :, cols] = w
            stat_ref[g, 0:1, cols] = m
            stat_ref[g, 1:2, cols] = jnp.sum(w, axis=0, keepdims=True)


def global_kernel(
    q_ref, shifted_ref, loss_ref, own_ref, on_ref, off_ref, held_ref, other_ref, w_ref, stat_ref,
    dp_ref, ds_ref, out_stat_ref, keep_ref, give_ref, do_ref,
):
    last = at_last_section()

    @pl.when(last)
    def _():
        do_ref[...] = loss_ref[...]

    @pl.when(jnp.logical_not(last))
    def _():
        do_ref[...] = shifted_ref[...]

    for g in range(KEY_HEADS):
        kc = g * HEAD_SIZE
        vc = WIDTH + kc
        qg = group_rows(q_ref, g)
        dog = group_rows(do_ref, g)
        t = dot(stacked((held_ref, other_ref), kc), qg, NT) * (SCALE * LOG2E)
        dpg = dot(stacked((held_ref, other_ref), vc), dog, NT)
        dpl = dot(stacked((own_ref, on_ref, off_ref), vc), dog, NT)
        dp_ref[g] = dpl
        partial_delta = jnp.sum(w_ref[g] * dpl, axis=0, keepdims=True)
        m_local = stat_ref[g, 0:1, :]
        m = jnp.maximum(m_local, jnp.max(t, axis=0, keepdims=True))
        shrink = jnp.exp2(m_local - m)
        w = jnp.exp2(t - m)
        total = shrink * stat_ref[g, 1:2, :] + jnp.sum(w, axis=0, keepdims=True)
        inv = 1.0 / total
        p = w * inv
        local_factor = shrink * inv
        delta = local_factor * partial_delta + jnp.sum(p * dpg, axis=0, keepdims=True)
        ds = (p * (dpg - delta) * SCALE).astype(BF)
        ds_ref[g] = ds
        out_stat_ref[g, 0:1, :] = local_factor
        out_stat_ref[g, 1:2, :] = delta
        cols = slice(kc, kc + HEAD_SIZE)
        for i, grad in enumerate((dot(ds, qg, NN), dot(p.astype(BF), dog, NN))):
            keep_ref[i, :, cols] = grad[:BLOCK_TOKENS]
            give_ref[i, :, cols] = grad[BLOCK_TOKENS:].astype(BF)


def local_ds(w_ref, dp_ref, stat_ref, g):
    p = w_ref[g] * stat_ref[g, 0:1, :]
    return p, (p * (dp_ref[g] - stat_ref[g, 1:2, :]) * SCALE).astype(BF)


def pairs_kernel(q_ref, do_ref, w_ref, dp_ref, stat_ref, g_own, g_on, g_off, ds_ref):
    toks = q_ref.shape[0]
    for g in range(KEY_HEADS):
        p, ds = local_ds(w_ref, dp_ref, stat_ref, g)
        ds_ref[g] = ds
        cols = slice(g * HEAD_SIZE, (g + 1) * HEAD_SIZE)
        grads = (dot(ds, group_rows(q_ref, g), NN), dot(p.astype(BF), group_rows(do_ref, g), NN))
        for i, grad in enumerate(grads):
            g_own[i, :, cols] = grad[:toks]
            g_on[i, :, cols] = grad[toks : 2 * toks].astype(BF)
            g_off[i, :, cols] = grad[2 * toks :].astype(BF)


def queries_kernel(
    own_ref, on_ref, off_ref, held_ref, other_ref, ds_local_ref, ds_global_ref, dq_ref
):
    toks = dq_ref.shape[0]
    for g in range(KEY_HEADS):
        keys = stacked((own_ref, on_ref, off_ref, held_ref, other_ref), g * HEAD_SIZE)
        dq = dot(keys, jnp.concatenate([ds_local_ref[g], ds_global_ref[g]], 0), TN).T
        for e in range(toks // BLOCK_TOKENS):
            for h in range(GROUP_HEADS):
                r = e * ROWS_E + h * BLOCK_TOKENS
                c = (g * GROUP_HEADS + h) * HEAD_SIZE
                dq_ref[e * BLOCK_TOKENS : (e + 1) * BLOCK_TOKENS, c : c + HEAD_SIZE] = (
                    dq[r : r + BLOCK_TOKENS].astype(BF)
                )


def finish_kernel(place_ref, g_own, r_on, r_off, half_ref, half_other_ref, out_ref):
    toks = g_own.shape[1]
    nb = toks // BLOCK_TOKENS
    core = lax.rem(lax.axis_index("seq"), 2)
    places = (place_ref[core], place_ref[1 - core])
    for i in range(2):
        for s in range(nb):
            rows = slice(s * BLOCK_TOKENS, (s + 1) * BLOCK_TOKENS)
            total = g_own[i, rows] + r_on[i, rows].astype(F32) + r_off[i, rows].astype(F32)
            for place, ref in zip(places, (half_ref, half_other_ref)):
                total = total + jnp.where(place == s, ref[i].astype(F32), 0.0)
            out_ref[rows, i * WIDTH : (i + 1) * WIDTH] = total.astype(BF)


def list_bias(random_table, pos, peers, nb):
    core = pos % 2
    step = jnp.arange(nb, dtype=jnp.int32)
    holders = (pos, pos + 1 - 2 * core, pos - 1 + 2 * core)
    cand_ids = jnp.concatenate([h * nb + step for h in holders])
    block_ids = pos * nb + step
    own_random = lax.dynamic_slice_in_dim(random_table, pos * nb, nb, 0)
    listed = jnp.sum((own_random[:, :, None, :] == cand_ids[None, None, :, None]).astype(F32), -1)
    inside = (cand_ids >= 0) & (cand_ids < peers * nb)
    window = (jnp.abs(cand_ids[None, :] - block_ids[:, None]) <= 1) & inside[None, :]
    times = listed + window[:, None, :].astype(F32)
    bias = jnp.where(times > 0, jnp.log2(jnp.maximum(times, 1.0)), NEG)
    return bias.reshape(nb, -1)


def body(queries, packed_key_value, incoming, loss_grad, global_blocks, random_blocks):
    toks = queries.shape[1]
    nb = toks // BLOCK_TOKENS
    rows = nb * ROWS_E
    sections = lax.axis_size("section")
    peers = lax.axis_size("seq")
    bits = peers.bit_length() - 1
    assert peers == 1 << bits and bits >= 1
    pos = lax.axis_index("seq")

    twin = [(i, i ^ 1) for i in range(peers)]
    side = [(i, i + 1) for i in range(1, peers - 1, 2)]
    side = side + [(j, i) for i, j in side]
    orders = (list(range(1, bits)), list(range(2, bits)) + [1])
    hops = [
        [(i, i ^ (1 << orders[i % 2][r])) for i in range(peers)] for r in range(bits - 1)
    ]

    def exchange(x, pairs, axis="seq"):
        return lax.ppermute(x, axis, pairs)

    q = queries[0]
    own = packed_key_value[0]
    on = exchange(own, twin)
    shifted = exchange(incoming[0], [(i, i - 1) for i in range(1, sections)], "section")
    table = jnp.concatenate([global_blocks // nb, global_blocks % nb], 0)
    (held,) = call(
        pick_kernel, [SMEM, HBM, VMEM],
        [shape(BLOCK_TOKENS, own.shape[1], dtype=BF)],
        (table, own, on), 10**6, [pltpu.SemaphoreType.DMA],
    )
    off = exchange(own, side)
    own, q, loss_grad = call(
        load_kernel, [HBM] * 3,
        [shape(*x.shape, dtype=BF) for x in (own, q, loss_grad)],
        (own, q, loss_grad), 10**7, [pltpu.SemaphoreType.DMA((3,))],
    )
    for hop in hops:
        held = held + exchange(held, hop)
    other = exchange(held, twin)

    bias = list_bias(random_blocks[0], pos, peers, nb)
    near = (own, on, off)
    w, stats = call(
        local_kernel, [SMEM] + [VMEM] * 4,
        [shape(KEY_HEADS, 3 * toks, rows), shape(KEY_HEADS, 8, rows)],
        (bias, q) + near, 3 * 10**9,
    )
    dp, ds, stats, keep, give, d_out = call(
        global_kernel, [VMEM] * 10,
        [
            shape(KEY_HEADS, 3 * toks, rows),
            shape(KEY_HEADS, GLOB_ROWS, rows, dtype=BF),
            shape(KEY_HEADS, 8, rows),
            shape(2, BLOCK_TOKENS, WIDTH),
            shape(2, BLOCK_TOKENS, WIDTH, dtype=BF),
            shape(*q.shape, dtype=BF),
        ],
        (q, shifted, loss_grad) + near + (held, other, w, stats), 3 * 10**9,
    )
    total = keep + exchange(give, twin).astype(F32)
    g_own, g_on, g_off, ds_local = call(
        pairs_kernel, [VMEM] * 5,
        [
            shape(2, toks, WIDTH),
            shape(2, toks, WIDTH, dtype=BF),
            shape(2, toks, WIDTH, dtype=BF),
            shape(KEY_HEADS, 3 * toks, rows, dtype=BF),
        ],
        (q, d_out, w, dp, stats), 3 * 10**9,
    )
    (dq,) = call(
        queries_kernel, [VMEM] * 7, [shape(*q.shape, dtype=BF)],
        near + (held, other, ds_local, ds), 2 * 10**9,
    )
    place = jnp.where(table[0] == pos, table[1], -1)
    r_on = exchange(g_on, twin)
    r_off = exchange(g_off, side)
    for hop in hops:
        total = total + exchange(total.astype(BF), hop).astype(F32)
    half = total.astype(BF)
    half_other = exchange(half, twin)
    (out,) = call(
        finish_kernel, [SMEM] + [VMEM] * 5, [shape(*own.shape, dtype=BF)],
        (place, g_own, r_on, r_off, half, half_other), 10**6,
    )
    return (dq[None], out[None])


def solution(mesh):
    in_specs = (
        P("section", "seq", None),
        P("section", "seq", None),
        P("section", "seq", None),
        P("seq", None),
        P("section", None),
        P("section", None, None, None),
    )
    out_specs = (P("section", "seq", None), P("section", "seq", None))
    return jax.shard_map(body, mesh=mesh, in_specs=in_specs, out_specs=out_specs, check_vma=False)
```

```python
import math

import jax
import jax.numpy as jnp
from jax import lax
from jax.experimental import pallas as pl
from jax.experimental.pallas import tpu as pltpu
from jax.sharding import PartitionSpec as P


KEY_HEADS = 4
HEAD_SIZE = 128
BLOCK_TOKENS = 64
GLOBAL_BLOCKS = 2
GROUP_HEADS = 6
SCALE = 1.0 / math.sqrt(HEAD_SIZE)
LOG2E = math.log2(math.e)
NEG = -1e30
WIDTH = KEY_HEADS * HEAD_SIZE
ROWS_E = GROUP_HEADS * BLOCK_TOKENS
GLOB_ROWS = GLOBAL_BLOCKS * BLOCK_TOKENS
NT = (((1,), (1,)), ((), ()))
NN = (((1,), (0,)), ((), ()))
TN = (((0,), (0,)), ((), ()))
F32 = jnp.float32
BF = jnp.bfloat16
HBM = pl.BlockSpec(memory_space=pltpu.HBM)
VMEM = pl.BlockSpec(memory_space=pltpu.VMEM)
SMEM = pl.BlockSpec(memory_space=pltpu.SMEM)


def dot(a, b, dims):
    return lax.dot_general(a, b, dims, preferred_element_type=F32)


def call(kernel, ins, outs, args, flops, scratch=()):
    return pl.pallas_call(
        kernel,
        in_specs=ins,
        out_specs=[VMEM] * len(outs),
        out_shape=outs,
        scratch_shapes=scratch,
        compiler_params=pltpu.CompilerParams(vmem_limit_bytes=24 << 20),
        cost_estimate=pl.CostEstimate(flops=flops, bytes_accessed=flops // 500, transcendentals=0),
    )(*args)


def shape(*dims, dtype=F32):
    return jax.ShapeDtypeStruct(dims, dtype)


def group_rows(ref, g):
    toks = ref.shape[0]
    parts = []
    for e in range(toks // BLOCK_TOKENS):
        for h in range(GROUP_HEADS):
            c = (g * GROUP_HEADS + h) * HEAD_SIZE
            parts.append(ref[e * BLOCK_TOKENS : (e + 1) * BLOCK_TOKENS, c : c + HEAD_SIZE])
    return jnp.concatenate(parts, 0)


def stacked(refs, c):
    return jnp.concatenate([ref[:, c : c + HEAD_SIZE] for ref in refs], 0)


def at_last_section():
    return lax.axis_index("section") == lax.axis_size("section") - 1


def load_kernel(a_ref, b_ref, c_ref, a_out, b_out, c_out, sems):
    copies = [
        pltpu.make_async_copy(src, dst, sems.at[i])
        for i, (src, dst) in enumerate(((a_ref, a_out), (b_ref, b_out), (c_ref, c_out)))
    ]
    for copy in copies:
        copy.start()
    for copy in copies:
        copy.wait()


def pick_kernel(table_ref, own_ref, on_ref, out_ref, sem):
    pos = lax.axis_index("seq")
    core = lax.rem(pos, 2)
    owner = table_ref[0, core]
    row = pl.multiple_of(table_ref[1, core] * BLOCK_TOKENS, BLOCK_TOKENS)
    mine = owner == pos
    theirs = owner == pos + 1 - 2 * core

    @pl.when(mine)
    def _():
        copy = pltpu.make_async_copy(own_ref.at[pl.ds(row, BLOCK_TOKENS)], out_ref, sem)
        copy.start()
        copy.wait()

    @pl.when(theirs)
    def _():
        out_ref[...] = on_ref[pl.ds(row, BLOCK_TOKENS), :]

    @pl.when(jnp.logical_not(mine | theirs))
    def _():
        out_ref[...] = jnp.zeros_like(out_ref)


def local_kernel(bias_ref, q_ref, own_ref, on_ref, off_ref, w_ref, stat_ref):
    toks = q_ref.shape[0]
    nb = toks // BLOCK_TOKENS
    ncand = 3 * nb
    for g in range(KEY_HEADS):
        keys = stacked((own_ref, on_ref, off_ref), g * HEAD_SIZE)
        s = dot(keys, group_rows(q_ref, g), NT)
        for e in range(nb):
            cols = slice(e * ROWS_E, (e + 1) * ROWS_E)
            t = jnp.concatenate(
                [
                    s[j * BLOCK_TOKENS : (j + 1) * BLOCK_TOKENS, cols] * (SCALE * LOG2E)
                    + bias_ref[e, g * ncand + j]
                    for j in range(ncand)
                ],
                0,
            )
            m = jnp.max(t, axis=0, keepdims=True)
            w = jnp.exp2(t - m)
            w_ref[g, :, cols] = w
            stat_ref[g, 0:1, cols] = m
            stat_ref[g, 1:2, cols] = jnp.sum(w, axis=0, keepdims=True)


def near_kernel(
    shifted_ref, loss_ref, own_ref, on_ref, off_ref, w_ref, stat_ref, dp_ref, out_stat_ref, do_ref
):
    last = at_last_section()

    @pl.when(last)
    def _():
        do_ref[...] = loss_ref[...]

    @pl.when(jnp.logical_not(last))
    def _():
        do_ref[...] = shifted_ref[...]

    for g in range(KEY_HEADS):
        vals = stacked((own_ref, on_ref, off_ref), WIDTH + g * HEAD_SIZE)
        dp = dot(vals, group_rows(do_ref, g), NT)
        dp_ref[g] = dp
        out_stat_ref[g, 0:2, :] = stat_ref[g, 0:2, :]
        out_stat_ref[g, 2:3, :] = jnp.sum(w_ref[g] * dp, axis=0, keepdims=True)


def global_kernel(
    q_ref, do_ref, held_ref, other_ref, stat_ref, ds_ref, out_stat_ref, keep_ref, give_ref
):
    for g in range(KEY_HEADS):
        kc = g * HEAD_SIZE
        qg = group_rows(q_ref, g)
        dog = group_rows(do_ref, g)
        t = dot(stacked((held_ref, other_ref), kc), qg, NT) * (SCALE * LOG2E)
        dp = dot(stacked((held_ref, other_ref), WIDTH + kc), dog, NT)
        m_local = stat_ref[g, 0:1, :]
        m = jnp.maximum(m_local, jnp.max(t, axis=0, keepdims=True))
        shrink = jnp.exp2(m_local - m)
        w = jnp.exp2(t - m)
        total = shrink * stat_ref[g, 1:2, :] + jnp.sum(w, axis=0, keepdims=True)
        inv = 1.0 / total
        p = w * inv
        local_factor = shrink * inv
        delta = local_factor * stat_ref[g, 2:3, :] + jnp.sum(p * dp, axis=0, keepdims=True)
        ds = (p * (dp - delta) * SCALE).astype(BF)
        ds_ref[g] = ds
        out_stat_ref[g, 0:1, :] = local_factor
        out_stat_ref[g, 1:2, :] = delta
        cols = slice(kc, kc + HEAD_SIZE)
        for i, grad in enumerate((dot(ds, qg, NN), dot(p.astype(BF), dog, NN))):
            keep_ref[i, :, cols] = grad[:BLOCK_TOKENS]
            give_ref[i, :, cols] = grad[BLOCK_TOKENS:].astype(BF)


def local_ds(w_ref, dp_ref, stat_ref, g):
    p = w_ref[g] * stat_ref[g, 0:1, :]
    return p, (p * (dp_ref[g] - stat_ref[g, 1:2, :]) * SCALE).astype(BF)


def pairs_kernel(q_ref, do_ref, w_ref, dp_ref, stat_ref, g_own, g_on, g_off, ds_ref):
    toks = q_ref.shape[0]
    for g in range(KEY_HEADS):
        p, ds = local_ds(w_ref, dp_ref, stat_ref, g)
        ds_ref[g] = ds
        cols = slice(g * HEAD_SIZE, (g + 1) * HEAD_SIZE)
        grads = (dot(ds, group_rows(q_ref, g), NN), dot(p.astype(BF), group_rows(do_ref, g), NN))
        for i, grad in enumerate(grads):
            g_own[i, :, cols] = grad[:toks]
            g_on[i, :, cols] = grad[toks : 2 * toks].astype(BF)
            g_off[i, :, cols] = grad[2 * toks :].astype(BF)


def queries_kernel(
    own_ref, on_ref, off_ref, held_ref, other_ref, ds_local_ref, ds_global_ref, dq_ref
):
    toks = dq_ref.shape[0]
    for g in range(KEY_HEADS):
        keys = stacked((own_ref, on_ref, off_ref, held_ref, other_ref), g * HEAD_SIZE)
        dq = dot(keys, jnp.concatenate([ds_local_ref[g], ds_global_ref[g]], 0), TN).T
        for e in range(toks // BLOCK_TOKENS):
            for h in range(GROUP_HEADS):
                r = e * ROWS_E + h * BLOCK_TOKENS
                c = (g * GROUP_HEADS + h) * HEAD_SIZE
                dq_ref[e * BLOCK_TOKENS : (e + 1) * BLOCK_TOKENS, c : c + HEAD_SIZE] = (
                    dq[r : r + BLOCK_TOKENS].astype(BF)
                )


def place_kernel(table_ref, out_ref):
    here = table_ref[0:1, :] == lax.axis_index("seq")
    out_ref[...] = jnp.where(here, table_ref[1:2, :], -1)


def finish_kernel(place_ref, g_own, r_on, r_off, half_ref, half_other_ref, out_ref):
    toks = g_own.shape[1]
    nb = toks // BLOCK_TOKENS
    core = lax.rem(lax.axis_index("seq"), 2)
    places = (place_ref[0, core], place_ref[0, 1 - core])
    for i in range(2):
        for s in range(nb):
            rows = slice(s * BLOCK_TOKENS, (s + 1) * BLOCK_TOKENS)
            total = g_own[i, rows] + r_on[i, rows].astype(F32) + r_off[i, rows].astype(F32)
            for place, ref in zip(places, (half_ref, half_other_ref)):
                total = total + jnp.where(place == s, ref[i].astype(F32), 0.0)
            out_ref[rows, i * WIDTH : (i + 1) * WIDTH] = total.astype(BF)


def list_bias(random_table, pos, peers, nb):
    core = pos % 2
    step = jnp.arange(nb, dtype=jnp.int32)
    holders = (pos, pos + 1 - 2 * core, pos - 1 + 2 * core)
    cand_ids = jnp.concatenate([h * nb + step for h in holders])
    block_ids = pos * nb + step
    own_random = lax.dynamic_slice_in_dim(random_table, pos * nb, nb, 0)
    listed = jnp.sum((own_random[:, :, None, :] == cand_ids[None, None, :, None]).astype(F32), -1)
    inside = (cand_ids >= 0) & (cand_ids < peers * nb)
    window = (jnp.abs(cand_ids[None, :] - block_ids[:, None]) <= 1) & inside[None, :]
    times = listed + window[:, None, :].astype(F32)
    bias = jnp.where(times > 0, jnp.log2(jnp.maximum(times, 1.0)), NEG)
    return bias.reshape(nb, -1)


def mask_rounds(bits):
    if bits < 3:
        return [[1 << b] for b in range(1, bits)]
    rounds = [[2, 4, 6]] + [[1 << b] for b in range(3, bits)]
    if bits > 3:
        rounds[-1] = [3 << (bits - 2)]
    return rounds


def body(queries, packed_key_value, incoming, loss_grad, global_blocks, random_blocks):
    toks = queries.shape[1]
    nb = toks // BLOCK_TOKENS
    rows = nb * ROWS_E
    sections = lax.axis_size("section")
    peers = lax.axis_size("seq")
    bits = peers.bit_length() - 1
    assert peers == 1 << bits and bits >= 1
    pos = lax.axis_index("seq")

    twin = [(i, i ^ 1) for i in range(peers)]
    side = [(i, i + 1) for i in range(1, peers - 1, 2)]
    side = side + [(j, i) for i, j in side]
    rounds = mask_rounds(bits)

    def flipped(mask):
        return [(i, i ^ mask) for i in range(peers)]

    def exchange(x, pairs, axis="seq"):
        return lax.ppermute(x, axis, pairs)

    q = queries[0]
    own = packed_key_value[0]
    on = exchange(own, twin)
    shifted = exchange(incoming[0], [(i, i - 1) for i in range(1, sections)], "section")
    table = jnp.concatenate([global_blocks // nb, global_blocks % nb], 0)
    (held,) = call(
        pick_kernel, [SMEM, HBM, VMEM],
        [shape(BLOCK_TOKENS, own.shape[1], dtype=BF)],
        (table, pltpu.with_memory_space_constraint(own, pltpu.HBM), on), 10**6, [pltpu.SemaphoreType.DMA],
    )
    off = exchange(own, side)
    own, q, loss_grad = call(
        load_kernel, [HBM] * 3,
        [shape(*x.shape, dtype=BF) for x in (own, q, loss_grad)],
        [pltpu.with_memory_space_constraint(x, pltpu.HBM) for x in (own, q, loss_grad)], 10**7, [pltpu.SemaphoreType.DMA((3,))],
    )
    for masks in rounds:
        got = [exchange(held, flipped(m)) for m in masks]
        held = sum(got, held)
    other = exchange(held, twin)

    bias = list_bias(random_blocks[0], pos, peers, nb)
    near = (own, on, off)
    w, stats = call(
        local_kernel, [SMEM] + [VMEM] * 4,
        [shape(KEY_HEADS, 3 * toks, rows), shape(KEY_HEADS, 8, rows)],
        (bias, q) + near, 3 * 10**9,
    )
    dp, stats, d_out = call(
        near_kernel, [VMEM] * 7,
        [
            shape(KEY_HEADS, 3 * toks, rows),
            shape(KEY_HEADS, 8, rows),
            shape(*q.shape, dtype=BF),
        ],
        (shifted, loss_grad) + near + (w, stats), 2 * 10**9,
    )
    ds, stats, keep, give = call(
        global_kernel, [VMEM] * 5,
        [
            shape(KEY_HEADS, GLOB_ROWS, rows, dtype=BF),
            shape(KEY_HEADS, 8, rows),
            shape(2, BLOCK_TOKENS, WIDTH),
            shape(2, BLOCK_TOKENS, WIDTH, dtype=BF),
        ],
        (q, d_out, held, other, stats), 2 * 10**9,
    )
    total = keep + exchange(give, twin).astype(F32)
    g_own, g_on, g_off, ds_local = call(
        pairs_kernel, [VMEM] * 5,
        [
            shape(2, toks, WIDTH),
            shape(2, toks, WIDTH, dtype=BF),
            shape(2, toks, WIDTH, dtype=BF),
            shape(KEY_HEADS, 3 * toks, rows, dtype=BF),
        ],
        (q, d_out, w, dp, stats), 3 * 10**9,
    )
    (dq,) = call(
        queries_kernel, [VMEM] * 7, [shape(*q.shape, dtype=BF)],
        near + (held, other, ds_local, ds), 2 * 10**9,
    )
    (place,) = call(
        place_kernel, [VMEM], [shape(1, GLOBAL_BLOCKS, dtype=jnp.int32)], (table,), 1000
    )
    r_on = exchange(g_on, twin)
    r_off = exchange(g_off, side)
    for masks in rounds:
        sent = total.astype(BF)
        got = [exchange(sent, flipped(m)) for m in masks]
        total = sum([x.astype(F32) for x in got], total)
    half = total.astype(BF)
    half_other = exchange(half, twin)
    (out,) = call(
        finish_kernel, [SMEM] + [VMEM] * 5, [shape(*own.shape, dtype=BF)],
        (place, g_own, r_on, r_off, half, half_other), 10**6,
    )
    return (dq[None], out[None])


def solution(mesh):
    in_specs = (
        P("section", "seq", None),
        P("section", "seq", None),
        P("section", "seq", None),
        P("seq", None),
        P("section", None),
        P("section", None, None, None),
    )
    out_specs = (P("section", "seq", None), P("section", "seq", None))
    return jax.shard_map(body, mesh=mesh, in_specs=in_specs, out_specs=out_specs, check_vma=False)
```

```python
import functools
import math

import jax
import jax.numpy as jnp
from jax import lax
from jax.experimental import pallas as pl
from jax.experimental.pallas import tpu as pltpu
from jax.sharding import PartitionSpec as P


KEY_HEADS = 4
HEAD_SIZE = 128
BLOCK_TOKENS = 64
GLOBAL_BLOCKS = 2
GROUP_HEADS = 6
SCALE = 1.0 / math.sqrt(HEAD_SIZE)
LOG2E = math.log2(math.e)
NEG = -1e30
WIDTH = KEY_HEADS * HEAD_SIZE
ROWS_E = GROUP_HEADS * BLOCK_TOKENS
GLOB_ROWS = GLOBAL_BLOCKS * BLOCK_TOKENS
NT = (((1,), (1,)), ((), ()))
NN = (((1,), (0,)), ((), ()))
TN = (((0,), (0,)), ((), ()))
F32 = jnp.float32
BF = jnp.bfloat16
HBM = pl.BlockSpec(memory_space=pltpu.HBM)
VMEM = pl.BlockSpec(memory_space=pltpu.VMEM)
SMEM = pl.BlockSpec(memory_space=pltpu.SMEM)


def dot(a, b, dims):
    return lax.dot_general(a, b, dims, preferred_element_type=F32)


def call(kernel, ins, outs, args, flops, scratch=(), out_specs=None, aliases={}):
    return pl.pallas_call(
        kernel,
        in_specs=ins,
        out_specs=out_specs or [VMEM] * len(outs),
        input_output_aliases=aliases,
        out_shape=outs,
        scratch_shapes=scratch,
        compiler_params=pltpu.CompilerParams(vmem_limit_bytes=24 << 20),
        cost_estimate=pl.CostEstimate(flops=flops, bytes_accessed=flops // 500, transcendentals=0),
    )(*args)


def shape(*dims, dtype=F32):
    return jax.ShapeDtypeStruct(dims, dtype)


def group_rows(ref, g):
    toks = ref.shape[0]
    parts = []
    for e in range(toks // BLOCK_TOKENS):
        for h in range(GROUP_HEADS):
            c = (g * GROUP_HEADS + h) * HEAD_SIZE
            parts.append(ref[e * BLOCK_TOKENS : (e + 1) * BLOCK_TOKENS, c : c + HEAD_SIZE])
    return jnp.concatenate(parts, 0)


def stacked(refs, c):
    return jnp.concatenate([ref[:, c : c + HEAD_SIZE] for ref in refs], 0)


def at_last_section():
    return lax.axis_index("section") == lax.axis_size("section") - 1


def load_kernel(a_ref, b_ref, a_out, b_out, sems):
    copies = [
        pltpu.make_async_copy(src, dst, sems.at[i])
        for i, (src, dst) in enumerate(((a_ref, a_out), (b_ref, b_out)))
    ]
    for copy in copies:
        copy.start()
    for copy in copies:
        copy.wait()


def pick_kernel(ids_ref, own_ref, keep_ref, give_ref, own_out, ids, sems):
    nb = own_ref.shape[0] // BLOCK_TOKENS
    pos = lax.axis_index("seq")
    core = lax.rem(pos, 2)
    fetch_ids = pltpu.make_async_copy(ids_ref, ids, sems.at[0])
    fetch_own = pltpu.make_async_copy(own_ref, own_out, sems.at[1])
    fetch_ids.start()
    fetch_own.start()
    fetch_ids.wait()
    fetch_own.wait()
    for which, out in ((core, keep_ref), (1 - core, give_ref)):
        block = ids[0, which]
        mine = lax.div(block, nb) == pos
        row = pl.multiple_of(lax.rem(block, nb) * BLOCK_TOKENS, BLOCK_TOKENS)

        @pl.when(mine)
        def _(out=out, row=row):
            out[...] = own_out[pl.ds(row, BLOCK_TOKENS), :]

        @pl.when(jnp.logical_not(mine))
        def _(out=out):
            out[...] = jnp.zeros_like(out)


def local_kernel(bias_ref, q_ref, own_ref, on_ref, off_ref, w_ref, stat_ref):
    toks = q_ref.shape[0]
    nb = toks // BLOCK_TOKENS
    ncand = 3 * nb
    for g in range(KEY_HEADS):
        keys = stacked((own_ref, on_ref, off_ref), g * HEAD_SIZE)
        s = dot(keys, group_rows(q_ref, g), NT)
        for e in range(nb):
            cols = slice(e * ROWS_E, (e + 1) * ROWS_E)
            t = jnp.concatenate(
                [
                    s[j * BLOCK_TOKENS : (j + 1) * BLOCK_TOKENS, cols] * (SCALE * LOG2E)
                    + bias_ref[e, g * ncand + j]
                    for j in range(ncand)
                ],
                0,
            )
            m = jnp.max(t, axis=0, keepdims=True)
            w = jnp.exp2(t - m)
            w_ref[g, :, cols] = w
            stat_ref[g, 0:1, cols] = m
            stat_ref[g, 1:2, cols] = jnp.sum(w, axis=0, keepdims=True)


def near_kernel(
    shifted_ref, loss_ref, own_ref, on_ref, off_ref, w_ref, stat_ref, dp_ref, out_stat_ref, do_ref
):
    last = at_last_section()

    @pl.when(last)
    def _():
        do_ref[...] = loss_ref[...]

    @pl.when(jnp.logical_not(last))
    def _():
        do_ref[...] = shifted_ref[...]

    for g in range(KEY_HEADS):
        vals = stacked((own_ref, on_ref, off_ref), WIDTH + g * HEAD_SIZE)
        dp = dot(vals, group_rows(do_ref, g), NT)
        dp_ref[g] = dp
        out_stat_ref[g, 0:2, :] = stat_ref[g, 0:2, :]
        out_stat_ref[g, 2:3, :] = jnp.sum(w_ref[g] * dp, axis=0, keepdims=True)


def global_kernel(
    q_ref, do_ref, held_ref, other_ref, stat_ref, ds_ref, out_stat_ref, keep_ref, give_ref
):
    def scores(g):
        kc = g * HEAD_SIZE
        qg = group_rows(q_ref, g)
        dog = group_rows(do_ref, g)
        t = dot(stacked((held_ref, other_ref), kc), qg, NT) * (SCALE * LOG2E)
        return qg, dog, t, dot(stacked((held_ref, other_ref), WIDTH + kc), dog, NT)

    def weights(g, t, dp):
        m_local = stat_ref[g, 0:1, :]
        m = jnp.maximum(m_local, jnp.max(t, axis=0, keepdims=True))
        shrink = jnp.exp2(m_local - m)
        w = jnp.exp2(t - m)
        total = shrink * stat_ref[g, 1:2, :] + jnp.sum(w, axis=0, keepdims=True)
        inv = 1.0 / total
        p = w * inv
        local_factor = shrink * inv
        delta = local_factor * stat_ref[g, 2:3, :] + jnp.sum(p * dp, axis=0, keepdims=True)
        ds = (p * (dp - delta) * SCALE).astype(BF)
        ds_ref[g] = ds
        out_stat_ref[g, 0:1, :] = local_factor
        out_stat_ref[g, 1:2, :] = delta
        return ds, p.astype(BF)

    def sums(g, ds, p, qg, dog):
        cols = slice(g * HEAD_SIZE, (g + 1) * HEAD_SIZE)
        for i, grad in enumerate((dot(ds, qg, NN), dot(p, dog, NN))):
            keep_ref[i, :, cols] = grad[:BLOCK_TOKENS]
            give_ref[i, :, cols] = grad[BLOCK_TOKENS:].astype(BF)

    first = scores(0)
    for g in range(KEY_HEADS):
        qg, dog, t, dp = first
        if g + 1 < KEY_HEADS:
            first = scores(g + 1)
        ds, p = weights(g, t, dp)
        sums(g, ds, p, qg, dog)


def local_ds(w_ref, dp_ref, stat_ref, g):
    p = w_ref[g] * stat_ref[g, 0:1, :]
    return p, (p * (dp_ref[g] - stat_ref[g, 1:2, :]) * SCALE).astype(BF)


def pairs_kernel(q_ref, do_ref, w_ref, dp_ref, stat_ref, g_own, g_on, g_off, ds_ref):
    toks = q_ref.shape[0]
    for g in range(KEY_HEADS):
        p, ds = local_ds(w_ref, dp_ref, stat_ref, g)
        ds_ref[g] = ds
        cols = slice(g * HEAD_SIZE, (g + 1) * HEAD_SIZE)
        grads = (dot(ds, group_rows(q_ref, g), NN), dot(p.astype(BF), group_rows(do_ref, g), NN))
        for i, grad in enumerate(grads):
            g_own[i, :, cols] = grad[:toks]
            g_on[i, :, cols] = grad[toks : 2 * toks].astype(BF)
            g_off[i, :, cols] = grad[2 * toks :].astype(BF)


def queries_kernel(
    own_ref, on_ref, off_ref, held_ref, other_ref, ds_local_ref, ds_global_ref, dq_ref
):
    toks = dq_ref.shape[0]
    for g in range(KEY_HEADS):
        keys = stacked((own_ref, on_ref, off_ref, held_ref, other_ref), g * HEAD_SIZE)
        dq = dot(keys, jnp.concatenate([ds_local_ref[g], ds_global_ref[g]], 0), TN).T
        for e in range(toks // BLOCK_TOKENS):
            for h in range(GROUP_HEADS):
                r = e * ROWS_E + h * BLOCK_TOKENS
                c = (g * GROUP_HEADS + h) * HEAD_SIZE
                dq_ref[e * BLOCK_TOKENS : (e + 1) * BLOCK_TOKENS, c : c + HEAD_SIZE] = (
                    dq[r : r + BLOCK_TOKENS].astype(BF)
                )


def place_kernel(nb, ids_ref, out_ref):
    slot = ids_ref[...] - lax.axis_index("seq") * nb
    out_ref[...] = jnp.where((slot >= 0) & (slot < nb), slot, -1)


def merge_kernel(place_ref, g_own, r_on, r_off, half_ref, base_ref, out_ref, rows_ref, sems):
    toks = g_own.shape[1]
    place = place_ref[0, lax.rem(lax.axis_index("seq"), 2)]
    copies = []
    for s in range(toks // BLOCK_TOKENS):
        rows = slice(s * BLOCK_TOKENS, (s + 1) * BLOCK_TOKENS)
        for i in range(2):
            total = g_own[i, rows] + r_on[i, rows].astype(F32) + r_off[i, rows].astype(F32)
            total = total + jnp.where(place == s, half_ref[i].astype(F32), 0.0)
            base_ref[i, rows] = total
            rows_ref[rows, i * WIDTH : (i + 1) * WIDTH] = total.astype(BF)
        copies.append(pltpu.make_async_copy(rows_ref.at[rows], out_ref.at[rows], sems.at[s]))
        copies[-1].start()
    for copy in copies:
        copy.wait()


def finish_kernel(place_ref, base_ref, half_ref, in_ref, out_ref, rows_ref, sem):
    place = place_ref[0, 1 - lax.rem(lax.axis_index("seq"), 2)]

    @pl.when(place >= 0)
    def _():
        rows = pl.ds(pl.multiple_of(place * BLOCK_TOKENS, BLOCK_TOKENS), BLOCK_TOKENS)
        for i in range(2):
            total = base_ref[i, rows, :] + half_ref[i].astype(F32)
            rows_ref[:, i * WIDTH : (i + 1) * WIDTH] = total.astype(BF)
        copy = pltpu.make_async_copy(rows_ref, out_ref.at[rows], sem)
        copy.start()
        copy.wait()


def list_bias(random_table, pos, peers, nb):
    core = pos % 2
    step = jnp.arange(nb, dtype=jnp.int32)
    holders = (pos, pos + 1 - 2 * core, pos - 1 + 2 * core)
    cand_ids = jnp.concatenate([h * nb + step for h in holders])
    block_ids = pos * nb + step
    own_random = lax.dynamic_slice_in_dim(random_table, pos * nb, nb, 0)
    listed = jnp.sum((own_random[:, :, None, :] == cand_ids[None, None, :, None]).astype(F32), -1)
    inside = (cand_ids >= 0) & (cand_ids < peers * nb)
    window = (jnp.abs(cand_ids[None, :] - block_ids[:, None]) <= 1) & inside[None, :]
    times = listed + window[:, None, :].astype(F32)
    bias = jnp.where(times > 0, jnp.log2(jnp.maximum(times, 1.0)), NEG)
    return bias.reshape(nb, -1)


def mask_rounds(bits):
    if bits < 3:
        return [[1 << b] for b in range(1, bits)]
    rounds = [[2, 4, 6]] + [[1 << b] for b in range(3, bits)]
    if bits > 3:
        rounds[-1] = [3 << (bits - 2)]
    return rounds


def body(queries, packed_key_value, incoming, loss_grad, global_blocks, random_blocks):
    toks = queries.shape[1]
    nb = toks // BLOCK_TOKENS
    rows = nb * ROWS_E
    sections = lax.axis_size("section")
    peers = lax.axis_size("seq")
    bits = peers.bit_length() - 1
    assert peers == 1 << bits and bits >= 1
    pos = lax.axis_index("seq")

    twin = [(i, i ^ 1) for i in range(peers)]
    side = [(i, i + 1) for i in range(1, peers - 1, 2)]
    side = side + [(j, i) for i, j in side]
    rounds = mask_rounds(bits)

    def flipped(mask):
        return [(i, i ^ mask) for i in range(peers)]

    def exchange(x, pairs, axis="seq"):
        return lax.ppermute(x, axis, pairs)

    q = queries[0]
    own = packed_key_value[0]
    shifted = exchange(incoming[0], [(i, i - 1) for i in range(1, sections)], "section")
    held, give, own_near = call(
        pick_kernel, [HBM] * 2,
        [shape(BLOCK_TOKENS, own.shape[1], dtype=BF)] * 2 + [shape(*own.shape, dtype=BF)],
        [pltpu.with_memory_space_constraint(x, pltpu.HBM) for x in (global_blocks, own)], 10**6,
        [pltpu.SMEM((1, GLOBAL_BLOCKS), jnp.int32), pltpu.SemaphoreType.DMA((2,))],
    )
    held = held + exchange(give, twin)
    on = exchange(own_near, twin)
    off = exchange(own_near, side)
    own = own_near
    q, loss_grad = call(
        load_kernel, [HBM] * 2, [shape(*x.shape, dtype=BF) for x in (q, loss_grad)],
        [pltpu.with_memory_space_constraint(x, pltpu.HBM) for x in (q, loss_grad)], 10**7,
        [pltpu.SemaphoreType.DMA((2,))],
    )
    for masks in rounds:
        got = [exchange(held, flipped(m)) for m in masks]
        held = sum(got, held)
    other = exchange(held, twin)

    bias = list_bias(random_blocks[0], pos, peers, nb)
    near = (own, on, off)
    w, stats = call(
        local_kernel, [SMEM] + [VMEM] * 4,
        [shape(KEY_HEADS, 3 * toks, rows), shape(KEY_HEADS, 8, rows)],
        (bias, q) + near, 3 * 10**9,
    )
    dp, stats, d_out = call(
        near_kernel, [VMEM] * 7,
        [
            shape(KEY_HEADS, 3 * toks, rows),
            shape(KEY_HEADS, 8, rows),
            shape(*q.shape, dtype=BF),
        ],
        (shifted, loss_grad) + near + (w, stats), 2 * 10**9,
    )
    ds, stats, keep, give = call(
        global_kernel, [VMEM] * 5,
        [
            shape(KEY_HEADS, GLOB_ROWS, rows, dtype=BF),
            shape(KEY_HEADS, 8, rows),
            shape(2, BLOCK_TOKENS, WIDTH),
            shape(2, BLOCK_TOKENS, WIDTH, dtype=BF),
        ],
        (q, d_out, held, other, stats), 2 * 10**9,
    )
    total = keep + exchange(give, twin).astype(F32)
    g_own, g_on, g_off, ds_local = call(
        pairs_kernel, [VMEM] * 5,
        [
            shape(2, toks, WIDTH),
            shape(2, toks, WIDTH, dtype=BF),
            shape(2, toks, WIDTH, dtype=BF),
            shape(KEY_HEADS, 3 * toks, rows, dtype=BF),
        ],
        (q, d_out, w, dp, stats), 3 * 10**9,
    )
    (dq,) = call(
        queries_kernel, [VMEM] * 7, [shape(*q.shape, dtype=BF)],
        near + (held, other, ds_local, ds), 2 * 10**9,
    )
    (place,) = call(
        functools.partial(place_kernel, nb), [VMEM],
        [shape(1, GLOBAL_BLOCKS, dtype=jnp.int32)], (global_blocks,), 1000,
    )
    r_on = exchange(g_on, twin)
    r_off = exchange(g_off, side)
    for masks in rounds:
        sent = total.astype(BF)
        got = [exchange(sent, flipped(m)) for m in masks]
        total = sum([x.astype(F32) for x in got], total)
    half = total.astype(BF)
    half_other = exchange(half, twin)
    base, out = call(
        merge_kernel, [SMEM] + [VMEM] * 4,
        [shape(2, toks, WIDTH), shape(*own.shape, dtype=BF)],
        (place, g_own, r_on, r_off, half), 10**6,
        [pltpu.VMEM(own.shape, BF), pltpu.SemaphoreType.DMA((nb,))], [VMEM, HBM],
    )
    (out,) = call(
        finish_kernel, [SMEM, VMEM, VMEM, HBM], [shape(*own.shape, dtype=BF)],
        (place, base, half_other, out), 10**6,
        [pltpu.VMEM((BLOCK_TOKENS, own.shape[1]), BF), pltpu.SemaphoreType.DMA], [HBM], {3: 0},
    )
    return (dq[None], out[None])


def solution(mesh):
    in_specs = (
        P("section", "seq", None),
        P("section", "seq", None),
        P("section", "seq", None),
        P("seq", None),
        P("section", None),
        P("section", None, None, None),
    )
    out_specs = (P("section", "seq", None), P("section", "seq", None))
    return jax.shard_map(body, mesh=mesh, in_specs=in_specs, out_specs=out_specs, check_vma=False)
```

```python
import functools
import math

import jax
import jax.numpy as jnp
from jax import lax
from jax.experimental import pallas as pl
from jax.experimental.pallas import tpu as pltpu
from jax.sharding import PartitionSpec as P


KEY_HEADS = 4
HEAD_SIZE = 128
BLOCK_TOKENS = 64
GLOBAL_BLOCKS = 2
GROUP_HEADS = 6
SCALE = 1.0 / math.sqrt(HEAD_SIZE)
LOG2E = math.log2(math.e)
NEG = -1e30
WIDTH = KEY_HEADS * HEAD_SIZE
ROWS_E = GROUP_HEADS * BLOCK_TOKENS
GLOB_ROWS = GLOBAL_BLOCKS * BLOCK_TOKENS
NT = (((1,), (1,)), ((), ()))
NN = (((1,), (0,)), ((), ()))
TN = (((0,), (0,)), ((), ()))
F32 = jnp.float32
BF = jnp.bfloat16
HBM = pl.BlockSpec(memory_space=pltpu.HBM)
VMEM = pl.BlockSpec(memory_space=pltpu.VMEM)
SMEM = pl.BlockSpec(memory_space=pltpu.SMEM)


def dot(a, b, dims):
    return lax.dot_general(a, b, dims, preferred_element_type=F32)


def call(kernel, ins, outs, args, flops, scratch=(), out_specs=None, aliases={}):
    return pl.pallas_call(
        kernel,
        in_specs=ins,
        out_specs=out_specs or [VMEM] * len(outs),
        input_output_aliases=aliases,
        out_shape=outs,
        scratch_shapes=scratch,
        compiler_params=pltpu.CompilerParams(vmem_limit_bytes=24 << 20),
        cost_estimate=pl.CostEstimate(flops=flops, bytes_accessed=flops // 500, transcendentals=0),
    )(*args)


def shape(*dims, dtype=F32):
    return jax.ShapeDtypeStruct(dims, dtype)


def group_rows(ref, g):
    toks = ref.shape[0]
    parts = []
    for e in range(toks // BLOCK_TOKENS):
        for h in range(GROUP_HEADS):
            c = (g * GROUP_HEADS + h) * HEAD_SIZE
            parts.append(ref[e * BLOCK_TOKENS : (e + 1) * BLOCK_TOKENS, c : c + HEAD_SIZE])
    return jnp.concatenate(parts, 0)


def stacked(refs, c):
    return jnp.concatenate([ref[:, c : c + HEAD_SIZE] for ref in refs], 0)


def at_last_section():
    return lax.axis_index("section") == lax.axis_size("section") - 1


def load_kernel(a_ref, b_ref, a_out, b_out, sems):
    copies = [
        pltpu.make_async_copy(src, dst, sems.at[i])
        for i, (src, dst) in enumerate(((a_ref, a_out), (b_ref, b_out)))
    ]
    for copy in copies:
        copy.start()
    for copy in copies:
        copy.wait()


def pick_kernel(ids_ref, own_ref, keep_ref, give_ref, own_out, ids, sems):
    nb = own_ref.shape[0] // BLOCK_TOKENS
    pos = lax.axis_index("seq")
    core = lax.rem(pos, 2)
    fetch_ids = pltpu.make_async_copy(ids_ref, ids, sems.at[0])
    fetch_own = pltpu.make_async_copy(own_ref, own_out, sems.at[1])
    fetch_ids.start()
    fetch_own.start()
    fetch_ids.wait()
    fetch_own.wait()
    for which, out in ((core, keep_ref), (1 - core, give_ref)):
        block = ids[0, which]
        mine = lax.div(block, nb) == pos
        row = pl.multiple_of(lax.rem(block, nb) * BLOCK_TOKENS, BLOCK_TOKENS)

        @pl.when(mine)
        def _(out=out, row=row):
            out[...] = own_out[pl.ds(row, BLOCK_TOKENS), :]

        @pl.when(jnp.logical_not(mine))
        def _(out=out):
            out[...] = jnp.zeros_like(out)


def listed_scores(s, bias_ref, e, first):
    cols = slice(e * ROWS_E, (e + 1) * ROWS_E)
    parts = [
        s[j * BLOCK_TOKENS : (j + 1) * BLOCK_TOKENS, cols] * (SCALE * LOG2E)
        + bias_ref[e, first + j]
        for j in range(s.shape[0] // BLOCK_TOKENS)
    ]
    return cols, jnp.concatenate(parts, 0)


def local_kernel(bias_ref, q_ref, own_ref, on_ref, w_ref, stat_ref):
    nb = q_ref.shape[0] // BLOCK_TOKENS
    for g in range(KEY_HEADS):
        s = dot(stacked((own_ref, on_ref), g * HEAD_SIZE), group_rows(q_ref, g), NT)
        for e in range(nb):
            cols, t = listed_scores(s, bias_ref, e, g * 3 * nb)
            m = jnp.max(t, axis=0, keepdims=True)
            w = jnp.exp2(t - m)
            w_ref[g, :, cols] = w
            stat_ref[g, 0:1, cols] = m
            stat_ref[g, 1:2, cols] = jnp.sum(w, axis=0, keepdims=True)


def far_kernel(bias_ref, q_ref, off_ref, stat_ref, w_ref, out_stat_ref):
    nb = q_ref.shape[0] // BLOCK_TOKENS
    for g in range(KEY_HEADS):
        s = dot(off_ref[:, g * HEAD_SIZE : (g + 1) * HEAD_SIZE], group_rows(q_ref, g), NT)
        for e in range(nb):
            cols, t = listed_scores(s, bias_ref, e, g * 3 * nb + 2 * nb)
            m_near = stat_ref[g, 0:1, cols]
            m = jnp.maximum(m_near, jnp.max(t, axis=0, keepdims=True))
            w = jnp.exp2(t - m)
            w_ref[g, :, cols] = w
            shrink = jnp.exp2(m_near - m)
            out_stat_ref[g, 0:1, cols] = m
            out_stat_ref[g, 1:2, cols] = shrink * stat_ref[g, 1:2, cols] + jnp.sum(
                w, axis=0, keepdims=True
            )
            out_stat_ref[g, 2:3, cols] = shrink


def near_kernel(
    shifted_ref, loss_ref, own_ref, on_ref, off_ref, w_ref, w_off_ref, stat_ref,
    dp_ref, dp_off_ref, out_stat_ref, do_ref,
):
    last = at_last_section()

    @pl.when(last)
    def _():
        do_ref[...] = loss_ref[...]

    @pl.when(jnp.logical_not(last))
    def _():
        do_ref[...] = shifted_ref[...]

    for g in range(KEY_HEADS):
        vc = WIDTH + g * HEAD_SIZE
        dog = group_rows(do_ref, g)
        dp = dot(stacked((own_ref, on_ref), vc), dog, NT)
        dp_off = dot(off_ref[:, vc : vc + HEAD_SIZE], dog, NT)
        dp_ref[g] = dp
        dp_off_ref[g] = dp_off
        out_stat_ref[g, 0:3, :] = stat_ref[g, 0:3, :]
        out_stat_ref[g, 3:4, :] = stat_ref[g, 2:3, :] * jnp.sum(
            w_ref[g] * dp, axis=0, keepdims=True
        ) + jnp.sum(w_off_ref[g] * dp_off, axis=0, keepdims=True)


def global_kernel(
    q_ref, do_ref, held_ref, other_ref, stat_ref, ds_ref, out_stat_ref, keep_ref, give_ref
):
    def scores(g):
        kc = g * HEAD_SIZE
        qg = group_rows(q_ref, g)
        dog = group_rows(do_ref, g)
        t = dot(stacked((held_ref, other_ref), kc), qg, NT) * (SCALE * LOG2E)
        return qg, dog, t, dot(stacked((held_ref, other_ref), WIDTH + kc), dog, NT)

    def weights(g, t, dp):
        m_local = stat_ref[g, 0:1, :]
        m = jnp.maximum(m_local, jnp.max(t, axis=0, keepdims=True))
        shrink = jnp.exp2(m_local - m)
        w = jnp.exp2(t - m)
        total = shrink * stat_ref[g, 1:2, :] + jnp.sum(w, axis=0, keepdims=True)
        inv = 1.0 / total
        p = w * inv
        local_factor = shrink * inv
        delta = local_factor * stat_ref[g, 3:4, :] + jnp.sum(p * dp, axis=0, keepdims=True)
        ds = (p * (dp - delta) * SCALE).astype(BF)
        ds_ref[g] = ds
        out_stat_ref[g, 0:1, :] = local_factor * stat_ref[g, 2:3, :]
        out_stat_ref[g, 2:3, :] = local_factor
        out_stat_ref[g, 1:2, :] = delta
        return ds, p.astype(BF)

    def sums(g, ds, p, qg, dog):
        cols = slice(g * HEAD_SIZE, (g + 1) * HEAD_SIZE)
        for i, grad in enumerate((dot(ds, qg, NN), dot(p, dog, NN))):
            keep_ref[i, :, cols] = grad[:BLOCK_TOKENS]
            give_ref[i, :, cols] = grad[BLOCK_TOKENS:].astype(BF)

    staged = [scores(g) for g in range(KEY_HEADS)]
    for g, (qg, dog, t, dp) in enumerate(staged):
        ds, p = weights(g, t, dp)
        sums(g, ds, p, qg, dog)


def pairs_kernel(
    q_ref, do_ref, w_ref, w_off_ref, dp_ref, dp_off_ref, stat_ref, g_own, g_on, g_off, ds_ref
):
    toks = q_ref.shape[0]
    for g in range(KEY_HEADS):
        delta = stat_ref[g, 1:2, :]
        ps, dss = [], []
        for factor, w, dp in ((0, w_ref, dp_ref), (2, w_off_ref, dp_off_ref)):
            p = w[g] * stat_ref[g, factor : factor + 1, :]
            ps.append(p.astype(BF))
            dss.append((p * (dp[g] - delta) * SCALE).astype(BF))
        p = jnp.concatenate(ps, 0)
        ds = jnp.concatenate(dss, 0)
        ds_ref[g] = ds
        cols = slice(g * HEAD_SIZE, (g + 1) * HEAD_SIZE)
        for i, grad in enumerate((dot(ds, group_rows(q_ref, g), NN), dot(p, group_rows(do_ref, g), NN))):
            g_own[i, :, cols] = grad[:toks]
            g_on[i, :, cols] = grad[toks : 2 * toks].astype(BF)
            g_off[i, :, cols] = grad[2 * toks :].astype(BF)


def queries_kernel(
    own_ref, on_ref, off_ref, held_ref, other_ref, ds_local_ref, ds_global_ref, dq_ref
):
    toks = dq_ref.shape[0]
    for g in range(KEY_HEADS):
        keys = stacked((own_ref, on_ref, off_ref, held_ref, other_ref), g * HEAD_SIZE)
        dq = dot(keys, jnp.concatenate([ds_local_ref[g], ds_global_ref[g]], 0), TN).T
        for e in range(toks // BLOCK_TOKENS):
            for h in range(GROUP_HEADS):
                r = e * ROWS_E + h * BLOCK_TOKENS
                c = (g * GROUP_HEADS + h) * HEAD_SIZE
                dq_ref[e * BLOCK_TOKENS : (e + 1) * BLOCK_TOKENS, c : c + HEAD_SIZE] = (
                    dq[r : r + BLOCK_TOKENS].astype(BF)
                )


def place_kernel(nb, ids_ref, out_ref):
    slot = ids_ref[...] - lax.axis_index("seq") * nb
    out_ref[...] = jnp.where((slot >= 0) & (slot < nb), slot, -1)


def merge_kernel(place_ref, g_own, r_on, r_off, half_ref, base_ref, out_ref, rows_ref, sems):
    toks = g_own.shape[1]
    place = place_ref[0, lax.rem(lax.axis_index("seq"), 2)]
    copies = []
    for s in range(toks // BLOCK_TOKENS):
        rows = slice(s * BLOCK_TOKENS, (s + 1) * BLOCK_TOKENS)
        for i in range(2):
            total = g_own[i, rows] + r_on[i, rows].astype(F32) + r_off[i, rows].astype(F32)
            total = total + jnp.where(place == s, half_ref[i].astype(F32), 0.0)
            base_ref[i, rows] = total
            rows_ref[rows, i * WIDTH : (i + 1) * WIDTH] = total.astype(BF)
        copies.append(pltpu.make_async_copy(rows_ref.at[rows], out_ref.at[rows], sems.at[s]))
        copies[-1].start()
    for copy in copies:
        copy.wait()


def finish_kernel(place_ref, base_ref, half_ref, in_ref, out_ref, rows_ref, sem):
    place = place_ref[0, 1 - lax.rem(lax.axis_index("seq"), 2)]

    @pl.when(place >= 0)
    def _():
        rows = pl.ds(pl.multiple_of(place * BLOCK_TOKENS, BLOCK_TOKENS), BLOCK_TOKENS)
        for i in range(2):
            total = base_ref[i, rows, :] + half_ref[i].astype(F32)
            rows_ref[:, i * WIDTH : (i + 1) * WIDTH] = total.astype(BF)
        copy = pltpu.make_async_copy(rows_ref, out_ref.at[rows], sem)
        copy.start()
        copy.wait()


def list_bias(random_table, pos, peers, nb):
    core = pos % 2
    step = jnp.arange(nb, dtype=jnp.int32)
    holders = (pos, pos + 1 - 2 * core, pos - 1 + 2 * core)
    cand_ids = jnp.concatenate([h * nb + step for h in holders])
    block_ids = pos * nb + step
    own_random = lax.dynamic_slice_in_dim(random_table, pos * nb, nb, 0)
    listed = jnp.sum((own_random[:, :, None, :] == cand_ids[None, None, :, None]).astype(F32), -1)
    inside = (cand_ids >= 0) & (cand_ids < peers * nb)
    window = (jnp.abs(cand_ids[None, :] - block_ids[:, None]) <= 1) & inside[None, :]
    times = listed + window[:, None, :].astype(F32)
    bias = jnp.where(times > 0, jnp.log2(jnp.maximum(times, 1.0)), NEG)
    return bias.reshape(nb, -1)


def mask_rounds(bits):
    if bits < 3:
        return [[1 << b] for b in range(1, bits)]
    rounds = [[2, 4, 6]] + [[1 << b] for b in range(3, bits)]
    if bits > 3:
        rounds[-1] = [3 << (bits - 2)]
    return rounds


def body(queries, packed_key_value, incoming, loss_grad, global_blocks, random_blocks):
    toks = queries.shape[1]
    nb = toks // BLOCK_TOKENS
    rows = nb * ROWS_E
    sections = lax.axis_size("section")
    peers = lax.axis_size("seq")
    bits = peers.bit_length() - 1
    assert peers == 1 << bits and bits >= 1
    pos = lax.axis_index("seq")

    twin = [(i, i ^ 1) for i in range(peers)]
    side = [(i, i + 1) for i in range(1, peers - 1, 2)]
    side = side + [(j, i) for i, j in side]
    rounds = mask_rounds(bits)

    def flipped(mask):
        return [(i, i ^ mask) for i in range(peers)]

    def exchange(x, pairs, axis="seq"):
        return lax.ppermute(x, axis, pairs)

    q = queries[0]
    own = packed_key_value[0]
    shifted = exchange(incoming[0], [(i, i - 1) for i in range(1, sections)], "section")
    held, give, own_near = call(
        pick_kernel, [HBM] * 2,
        [shape(BLOCK_TOKENS, own.shape[1], dtype=BF)] * 2 + [shape(*own.shape, dtype=BF)],
        [pltpu.with_memory_space_constraint(x, pltpu.HBM) for x in (global_blocks, own)], 10**6,
        [pltpu.SMEM((1, GLOBAL_BLOCKS), jnp.int32), pltpu.SemaphoreType.DMA((2,))],
    )
    held = held + exchange(give, twin)
    on = exchange(own_near, twin)
    off = exchange(own_near, side)
    own = own_near
    q, loss_grad = call(
        load_kernel, [HBM] * 2, [shape(*x.shape, dtype=BF) for x in (q, loss_grad)],
        [pltpu.with_memory_space_constraint(x, pltpu.HBM) for x in (q, loss_grad)], 10**7,
        [pltpu.SemaphoreType.DMA((2,))],
    )
    for masks in rounds:
        got = [exchange(held, flipped(m)) for m in masks]
        held = sum(got, held)
    other = exchange(held, twin)

    bias = list_bias(random_blocks[0], pos, peers, nb)
    near = (own, on, off)
    w, stats = call(
        local_kernel, [SMEM] + [VMEM] * 3,
        [shape(KEY_HEADS, 2 * toks, rows), shape(KEY_HEADS, 8, rows)],
        (bias, q, own, on), 2 * 10**9,
    )
    w_off, stats = call(
        far_kernel, [SMEM] + [VMEM] * 3,
        [shape(KEY_HEADS, toks, rows), shape(KEY_HEADS, 8, rows)],
        (bias, q, off, stats), 10**9,
    )
    dp, dp_off, stats, d_out = call(
        near_kernel, [VMEM] * 8,
        [
            shape(KEY_HEADS, 2 * toks, rows),
            shape(KEY_HEADS, toks, rows),
            shape(KEY_HEADS, 8, rows),
            shape(*q.shape, dtype=BF),
        ],
        (shifted, loss_grad) + near + (w, w_off, stats), 2 * 10**9,
    )
    ds, stats, keep, give = call(
        global_kernel, [VMEM] * 5,
        [
            shape(KEY_HEADS, GLOB_ROWS, rows, dtype=BF),
            shape(KEY_HEADS, 8, rows),
            shape(2, BLOCK_TOKENS, WIDTH),
            shape(2, BLOCK_TOKENS, WIDTH, dtype=BF),
        ],
        (q, d_out, held, other, stats), 2 * 10**9,
    )
    total = keep + exchange(give, twin).astype(F32)
    g_own, g_on, g_off, ds_local = call(
        pairs_kernel, [VMEM] * 7,
        [
            shape(2, toks, WIDTH),
            shape(2, toks, WIDTH, dtype=BF),
            shape(2, toks, WIDTH, dtype=BF),
            shape(KEY_HEADS, 3 * toks, rows, dtype=BF),
        ],
        (q, d_out, w, w_off, dp, dp_off, stats), 3 * 10**9,
    )
    (dq,) = call(
        queries_kernel, [VMEM] * 7, [shape(*q.shape, dtype=BF)],
        near + (held, other, ds_local, ds), 2 * 10**9,
    )
    (place,) = call(
        functools.partial(place_kernel, nb), [VMEM],
        [shape(1, GLOBAL_BLOCKS, dtype=jnp.int32)], (global_blocks,), 1000,
    )
    r_on = exchange(g_on, twin)
    r_off = exchange(g_off, side)
    for masks in rounds:
        sent = total.astype(BF)
        got = [exchange(sent, flipped(m)) for m in masks]
        total = sum([x.astype(F32) for x in got], total)
    half = total.astype(BF)
    half_other = exchange(half, twin)
    base, out = call(
        merge_kernel, [SMEM] + [VMEM] * 4,
        [shape(2, toks, WIDTH), shape(*own.shape, dtype=BF)],
        (place, g_own, r_on, r_off, half), 10**6,
        [pltpu.VMEM(own.shape, BF), pltpu.SemaphoreType.DMA((nb,))], [VMEM, HBM],
    )
    (out,) = call(
        finish_kernel, [SMEM, VMEM, VMEM, HBM], [shape(*own.shape, dtype=BF)],
        (place, base, half_other, out), 10**6,
        [pltpu.VMEM((BLOCK_TOKENS, own.shape[1]), BF), pltpu.SemaphoreType.DMA], [HBM], {3: 0},
    )
    return (dq[None], out[None])


def solution(mesh):
    in_specs = (
        P("section", "seq", None),
        P("section", "seq", None),
        P("section", "seq", None),
        P("seq", None),
        P("section", None),
        P("section", None, None, None),
    )
    out_specs = (P("section", "seq", None), P("section", "seq", None))
    return jax.shard_map(body, mesh=mesh, in_specs=in_specs, out_specs=out_specs, check_vma=False)
```

```python
import functools
import math

import jax
import jax.numpy as jnp
from jax import lax
from jax.experimental import pallas as pl
from jax.experimental.pallas import tpu as pltpu
from jax.sharding import PartitionSpec as P


KEY_HEADS = 4
HEAD_SIZE = 128
BLOCK_TOKENS = 64
GLOBAL_BLOCKS = 2
GROUP_HEADS = 6
SCALE = 1.0 / math.sqrt(HEAD_SIZE)
LOG2E = math.log2(math.e)
NEG = -1e30
WIDTH = KEY_HEADS * HEAD_SIZE
ROWS_E = GROUP_HEADS * BLOCK_TOKENS
GLOB_ROWS = GLOBAL_BLOCKS * BLOCK_TOKENS
NT = (((1,), (1,)), ((), ()))
NN = (((1,), (0,)), ((), ()))
TN = (((0,), (0,)), ((), ()))
F32 = jnp.float32
BF = jnp.bfloat16
HBM = pl.BlockSpec(memory_space=pltpu.HBM)
VMEM = pl.BlockSpec(memory_space=pltpu.VMEM)
SMEM = pl.BlockSpec(memory_space=pltpu.SMEM)


def dot(a, b, dims):
    return lax.dot_general(a, b, dims, preferred_element_type=F32)


def call(kernel, ins, outs, args, flops, scratch=(), out_specs=None, aliases={}):
    return pl.pallas_call(
        kernel,
        in_specs=ins,
        out_specs=out_specs or [VMEM] * len(outs),
        input_output_aliases=aliases,
        out_shape=outs,
        scratch_shapes=scratch,
        compiler_params=pltpu.CompilerParams(vmem_limit_bytes=24 << 20),
        cost_estimate=pl.CostEstimate(flops=flops, bytes_accessed=flops // 500, transcendentals=0),
    )(*args)


def shape(*dims, dtype=F32):
    return jax.ShapeDtypeStruct(dims, dtype)


def group_rows(ref, g):
    toks = ref.shape[0]
    parts = []
    for e in range(toks // BLOCK_TOKENS):
        for h in range(GROUP_HEADS):
            c = (g * GROUP_HEADS + h) * HEAD_SIZE
            parts.append(ref[e * BLOCK_TOKENS : (e + 1) * BLOCK_TOKENS, c : c + HEAD_SIZE])
    return jnp.concatenate(parts, 0)


def stacked(refs, c):
    return jnp.concatenate([ref[:, c : c + HEAD_SIZE] for ref in refs], 0)


def at_last_section():
    return lax.axis_index("section") == lax.axis_size("section") - 1


def load_kernel(a_ref, b_ref, a_out, b_out, sems):
    copies = [
        pltpu.make_async_copy(src, dst, sems.at[i])
        for i, (src, dst) in enumerate(((a_ref, a_out), (b_ref, b_out)))
    ]
    for copy in copies:
        copy.start()
    for copy in copies:
        copy.wait()


def pick_kernel(ids_ref, own_ref, keep_ref, give_ref, own_out, ids, sems):
    nb = own_ref.shape[0] // BLOCK_TOKENS
    pos = lax.axis_index("seq")
    core = lax.rem(pos, 2)
    fetch_ids = pltpu.make_async_copy(ids_ref, ids, sems.at[0])
    fetch_own = pltpu.make_async_copy(own_ref, own_out, sems.at[1])
    fetch_ids.start()
    fetch_own.start()
    keep_ref[...] = jnp.zeros_like(keep_ref)
    give_ref[...] = jnp.zeros_like(give_ref)
    fetch_ids.wait()
    fetch_own.wait()
    for which, out in ((core, keep_ref), (1 - core, give_ref)):
        block = ids[0, which]
        row = pl.multiple_of(lax.rem(block, nb) * BLOCK_TOKENS, BLOCK_TOKENS)

        @pl.when(lax.div(block, nb) == pos)
        def _(out=out, row=row):
            out[...] = own_out[pl.ds(row, BLOCK_TOKENS), :]


def listed_scores(s, bias_ref, e, first):
    cols = slice(e * ROWS_E, (e + 1) * ROWS_E)
    parts = [
        s[j * BLOCK_TOKENS : (j + 1) * BLOCK_TOKENS, cols] * (SCALE * LOG2E)
        + bias_ref[e, first + j]
        for j in range(s.shape[0] // BLOCK_TOKENS)
    ]
    return cols, jnp.concatenate(parts, 0)


def local_kernel(bias_ref, q_ref, own_ref, on_ref, w_ref, stat_ref):
    nb = q_ref.shape[0] // BLOCK_TOKENS
    for g in range(KEY_HEADS):
        s = dot(stacked((own_ref, on_ref), g * HEAD_SIZE), group_rows(q_ref, g), NT)
        for e in range(nb):
            cols, t = listed_scores(s, bias_ref, e, g * 3 * nb)
            m = jnp.max(t, axis=0, keepdims=True)
            w = jnp.exp2(t - m)
            w_ref[g, :, cols] = w
            stat_ref[g, 0:1, cols] = m
            stat_ref[g, 1:2, cols] = jnp.sum(w, axis=0, keepdims=True)


def far_kernel(bias_ref, q_ref, off_ref, stat_ref, w_ref, out_stat_ref):
    nb = q_ref.shape[0] // BLOCK_TOKENS
    for g in range(KEY_HEADS):
        s = dot(off_ref[:, g * HEAD_SIZE : (g + 1) * HEAD_SIZE], group_rows(q_ref, g), NT)
        for e in range(nb):
            cols, t = listed_scores(s, bias_ref, e, g * 3 * nb + 2 * nb)
            m_near = stat_ref[g, 0:1, cols]
            m = jnp.maximum(m_near, jnp.max(t, axis=0, keepdims=True))
            w = jnp.exp2(t - m)
            w_ref[g, :, cols] = w
            shrink = jnp.exp2(m_near - m)
            out_stat_ref[g, 0:1, cols] = m
            out_stat_ref[g, 1:2, cols] = shrink * stat_ref[g, 1:2, cols] + jnp.sum(
                w, axis=0, keepdims=True
            )
            out_stat_ref[g, 2:3, cols] = shrink


def near_kernel(
    shifted_ref, loss_ref, own_ref, on_ref, off_ref, w_ref, w_off_ref, stat_ref,
    dp_ref, dp_off_ref, out_stat_ref, do_ref,
):
    last = at_last_section()

    @pl.when(last)
    def _():
        do_ref[...] = loss_ref[...]

    @pl.when(jnp.logical_not(last))
    def _():
        do_ref[...] = shifted_ref[...]

    for g in range(KEY_HEADS):
        vc = WIDTH + g * HEAD_SIZE
        dog = group_rows(do_ref, g)
        dp = dot(stacked((own_ref, on_ref), vc), dog, NT)
        dp_off = dot(off_ref[:, vc : vc + HEAD_SIZE], dog, NT)
        dp_ref[g] = dp
        dp_off_ref[g] = dp_off
        out_stat_ref[g, 0:3, :] = stat_ref[g, 0:3, :]
        out_stat_ref[g, 3:4, :] = stat_ref[g, 2:3, :] * jnp.sum(
            w_ref[g] * dp, axis=0, keepdims=True
        ) + jnp.sum(w_off_ref[g] * dp_off, axis=0, keepdims=True)


def global_kernel(
    q_ref, do_ref, held_ref, other_ref, stat_ref, ds_ref, out_stat_ref, keep_ref, give_ref
):
    def scores(g):
        kc = g * HEAD_SIZE
        qg = group_rows(q_ref, g)
        dog = group_rows(do_ref, g)
        t = dot(stacked((held_ref, other_ref), kc), qg, NT) * (SCALE * LOG2E)
        return qg, dog, t, dot(stacked((held_ref, other_ref), WIDTH + kc), dog, NT)

    def weights(g, t, dp):
        m_local = stat_ref[g, 0:1, :]
        m = jnp.maximum(m_local, jnp.max(t, axis=0, keepdims=True))
        shrink = jnp.exp2(m_local - m)
        w = jnp.exp2(t - m)
        total = shrink * stat_ref[g, 1:2, :] + jnp.sum(w, axis=0, keepdims=True)
        inv = 1.0 / total
        p = w * inv
        local_factor = shrink * inv
        delta = local_factor * stat_ref[g, 3:4, :] + jnp.sum(p * dp, axis=0, keepdims=True)
        ds = (p * (dp - delta) * SCALE).astype(BF)
        ds_ref[g] = ds
        out_stat_ref[g, 0:1, :] = local_factor * stat_ref[g, 2:3, :]
        out_stat_ref[g, 2:3, :] = local_factor
        out_stat_ref[g, 1:2, :] = delta
        return ds, p.astype(BF)

    def sums(g, ds, p, qg, dog):
        cols = slice(g * HEAD_SIZE, (g + 1) * HEAD_SIZE)
        for i, grad in enumerate((dot(ds, qg, NN), dot(p, dog, NN))):
            keep_ref[i, :, cols] = grad[:BLOCK_TOKENS]
            give_ref[i, :, cols] = grad[BLOCK_TOKENS:].astype(BF)

    staged = [scores(g) for g in range(KEY_HEADS)]
    for g, (qg, dog, t, dp) in enumerate(staged):
        ds, p = weights(g, t, dp)
        sums(g, ds, p, qg, dog)


def pairs_kernel(
    q_ref, do_ref, w_ref, w_off_ref, dp_ref, dp_off_ref, stat_ref, g_own, g_on, g_off, ds_ref
):
    toks = q_ref.shape[0]
    for g in range(KEY_HEADS):
        delta = stat_ref[g, 1:2, :]
        ps, dss = [], []
        for factor, w, dp in ((0, w_ref, dp_ref), (2, w_off_ref, dp_off_ref)):
            p = w[g] * stat_ref[g, factor : factor + 1, :]
            ps.append(p.astype(BF))
            dss.append((p * (dp[g] - delta) * SCALE).astype(BF))
        p = jnp.concatenate(ps, 0)
        ds = jnp.concatenate(dss, 0)
        ds_ref[g] = ds
        cols = slice(g * HEAD_SIZE, (g + 1) * HEAD_SIZE)
        for i, grad in enumerate((dot(ds, group_rows(q_ref, g), NN), dot(p, group_rows(do_ref, g), NN))):
            g_own[i, :, cols] = grad[:toks]
            g_on[i, :, cols] = grad[toks : 2 * toks].astype(BF)
            g_off[i, :, cols] = grad[2 * toks :].astype(BF)


def queries_kernel(
    own_ref, on_ref, off_ref, held_ref, other_ref, ds_local_ref, ds_global_ref, dq_ref
):
    toks = dq_ref.shape[0]
    for g in range(KEY_HEADS):
        keys = stacked((own_ref, on_ref, off_ref, held_ref, other_ref), g * HEAD_SIZE)
        dq = dot(keys, jnp.concatenate([ds_local_ref[g], ds_global_ref[g]], 0), TN).T
        for e in range(toks // BLOCK_TOKENS):
            for h in range(GROUP_HEADS):
                r = e * ROWS_E + h * BLOCK_TOKENS
                c = (g * GROUP_HEADS + h) * HEAD_SIZE
                dq_ref[e * BLOCK_TOKENS : (e + 1) * BLOCK_TOKENS, c : c + HEAD_SIZE] = (
                    dq[r : r + BLOCK_TOKENS].astype(BF)
                )


def place_kernel(nb, ids_ref, out_ref):
    slot = ids_ref[...] - lax.axis_index("seq") * nb
    out_ref[...] = jnp.where((slot >= 0) & (slot < nb), slot, -1)


def merge_kernel(place_ref, g_own, r_on, r_off, half_ref, base_ref, out_ref, rows_ref, sems):
    toks = g_own.shape[1]
    place = place_ref[0, lax.rem(lax.axis_index("seq"), 2)]
    copies = []
    for s in range(toks // BLOCK_TOKENS):
        rows = slice(s * BLOCK_TOKENS, (s + 1) * BLOCK_TOKENS)
        for i in range(2):
            total = g_own[i, rows] + r_on[i, rows].astype(F32) + r_off[i, rows].astype(F32)
            total = total + jnp.where(place == s, half_ref[i].astype(F32), 0.0)
            base_ref[i, rows] = total
            rows_ref[rows, i * WIDTH : (i + 1) * WIDTH] = total.astype(BF)
        copies.append(pltpu.make_async_copy(rows_ref.at[rows], out_ref.at[rows], sems.at[s]))
        copies[-1].start()
    for copy in copies:
        copy.wait()


def finish_kernel(place_ref, base_ref, half_ref, in_ref, out_ref, rows_ref, sem):
    place = place_ref[0, 1 - lax.rem(lax.axis_index("seq"), 2)]

    @pl.when(place >= 0)
    def _():
        rows = pl.ds(pl.multiple_of(place * BLOCK_TOKENS, BLOCK_TOKENS), BLOCK_TOKENS)
        for i in range(2):
            total = base_ref[i, rows, :] + half_ref[i].astype(F32)
            rows_ref[:, i * WIDTH : (i + 1) * WIDTH] = total.astype(BF)
        copy = pltpu.make_async_copy(rows_ref, out_ref.at[rows], sem)
        copy.start()
        copy.wait()


def list_bias(random_table, pos, peers, nb):
    core = pos % 2
    step = jnp.arange(nb, dtype=jnp.int32)
    holders = (pos, pos + 1 - 2 * core, pos - 1 + 2 * core)
    cand_ids = jnp.concatenate([h * nb + step for h in holders])
    block_ids = pos * nb + step
    own_random = lax.dynamic_slice_in_dim(random_table, pos * nb, nb, 0)
    listed = jnp.sum((own_random[:, :, None, :] == cand_ids[None, None, :, None]).astype(F32), -1)
    inside = (cand_ids >= 0) & (cand_ids < peers * nb)
    window = (jnp.abs(cand_ids[None, :] - block_ids[:, None]) <= 1) & inside[None, :]
    times = listed + window[:, None, :].astype(F32)
    bias = jnp.where(times > 0, jnp.log2(jnp.maximum(times, 1.0)), NEG)
    return bias.reshape(nb, -1)


def mask_rounds(bits):
    if bits < 3:
        return [[1 << b] for b in range(1, bits)]
    rounds = [[2, 4, 6]] + [[1 << b] for b in range(3, bits)]
    if bits > 3:
        rounds[-1] = [3 << (bits - 2)]
    return rounds


def body(queries, packed_key_value, incoming, loss_grad, global_blocks, random_blocks):
    toks = queries.shape[1]
    nb = toks // BLOCK_TOKENS
    rows = nb * ROWS_E
    sections = lax.axis_size("section")
    peers = lax.axis_size("seq")
    bits = peers.bit_length() - 1
    assert peers == 1 << bits and bits >= 1
    pos = lax.axis_index("seq")

    twin = [(i, i ^ 1) for i in range(peers)]
    side = [(i, i + 1) for i in range(1, peers - 1, 2)]
    side = side + [(j, i) for i, j in side]
    rounds = mask_rounds(bits)

    def flipped(mask):
        return [(i, i ^ mask) for i in range(peers)]

    def exchange(x, pairs, axis="seq"):
        return lax.ppermute(x, axis, pairs)

    q = queries[0]
    own = packed_key_value[0]
    shifted = exchange(incoming[0], [(i, i - 1) for i in range(1, sections)], "section")
    held, give, own_near = call(
        pick_kernel, [HBM] * 2,
        [shape(BLOCK_TOKENS, own.shape[1], dtype=BF)] * 2 + [shape(*own.shape, dtype=BF)],
        [pltpu.with_memory_space_constraint(x, pltpu.HBM) for x in (global_blocks, own)], 10**6,
        [pltpu.SMEM((1, GLOBAL_BLOCKS), jnp.int32), pltpu.SemaphoreType.DMA((2,))],
    )
    held = held + exchange(give, twin)
    on = exchange(own_near, twin)
    off = exchange(own_near, side)
    own = own_near
    q, loss_grad = call(
        load_kernel, [HBM] * 2, [shape(*x.shape, dtype=BF) for x in (q, loss_grad)],
        [pltpu.with_memory_space_constraint(x, pltpu.HBM) for x in (q, loss_grad)], 10**7,
        [pltpu.SemaphoreType.DMA((2,))],
    )
    for masks in rounds:
        got = [exchange(held, flipped(m)) for m in masks]
        held = sum(got, held)
    other = exchange(held, twin)

    bias = list_bias(random_blocks[0], pos, peers, nb)
    near = (own, on, off)
    w, stats = call(
        local_kernel, [SMEM] + [VMEM] * 3,
        [shape(KEY_HEADS, 2 * toks, rows), shape(KEY_HEADS, 8, rows)],
        (bias, q, own, on), 2 * 10**9,
    )
    w_off, stats = call(
        far_kernel, [SMEM] + [VMEM] * 3,
        [shape(KEY_HEADS, toks, rows), shape(KEY_HEADS, 8, rows)],
        (bias, q, off, stats), 10**9,
    )
    dp, dp_off, stats, d_out = call(
        near_kernel, [VMEM] * 8,
        [
            shape(KEY_HEADS, 2 * toks, rows),
            shape(KEY_HEADS, toks, rows),
            shape(KEY_HEADS, 8, rows),
            shape(*q.shape, dtype=BF),
        ],
        (shifted, loss_grad) + near + (w, w_off, stats), 2 * 10**9,
    )
    ds, stats, keep, give = call(
        global_kernel, [VMEM] * 5,
        [
            shape(KEY_HEADS, GLOB_ROWS, rows, dtype=BF),
            shape(KEY_HEADS, 8, rows),
            shape(2, BLOCK_TOKENS, WIDTH),
            shape(2, BLOCK_TOKENS, WIDTH, dtype=BF),
        ],
        (q, d_out, held, other, stats), 2 * 10**9,
    )
    total = keep + exchange(give, twin).astype(F32)
    g_own, g_on, g_off, ds_local = call(
        pairs_kernel, [VMEM] * 7,
        [
            shape(2, toks, WIDTH),
            shape(2, toks, WIDTH, dtype=BF),
            shape(2, toks, WIDTH, dtype=BF),
            shape(KEY_HEADS, 3 * toks, rows, dtype=BF),
        ],
        (q, d_out, w, w_off, dp, dp_off, stats), 3 * 10**9,
    )
    (dq,) = call(
        queries_kernel, [VMEM] * 7, [shape(*q.shape, dtype=BF)],
        near + (held, other, ds_local, ds), 2 * 10**9,
    )
    (place,) = call(
        functools.partial(place_kernel, nb), [VMEM],
        [shape(1, GLOBAL_BLOCKS, dtype=jnp.int32)], (global_blocks,), 1000,
    )
    r_on = exchange(g_on, twin)
    r_off = exchange(g_off, side)
    for masks in rounds:
        sent = total.astype(BF)
        got = [exchange(sent, flipped(m)) for m in masks]
        total = sum([x.astype(F32) for x in got], total)
    half = total.astype(BF)
    half_other = exchange(half, twin)
    base, out = call(
        merge_kernel, [SMEM] + [VMEM] * 4,
        [shape(2, toks, WIDTH), shape(*own.shape, dtype=BF)],
        (place, g_own, r_on, r_off, half), 10**6,
        [pltpu.VMEM(own.shape, BF), pltpu.SemaphoreType.DMA((nb,))], [VMEM, HBM],
    )
    (out,) = call(
        finish_kernel, [SMEM, VMEM, VMEM, HBM], [shape(*own.shape, dtype=BF)],
        (place, base, half_other, out), 10**6,
        [pltpu.VMEM((BLOCK_TOKENS, own.shape[1]), BF), pltpu.SemaphoreType.DMA], [HBM], {3: 0},
    )
    return (dq[None], out[None])


def solution(mesh):
    in_specs = (
        P("section", "seq", None),
        P("section", "seq", None),
        P("section", "seq", None),
        P("seq", None),
        P("section", None),
        P("section", None, None, None),
    )
    out_specs = (P("section", "seq", None), P("section", "seq", None))
    return jax.shard_map(body, mesh=mesh, in_specs=in_specs, out_specs=out_specs, check_vma=False)
```
